256 devices in a mesh: rep: 128 (over z, y, x_hi, core), shard: 2 (over x_lo).
Axes of the slice: x: 4 (x_hi: 2, x_lo: 2; x = x_hi * 2 + x_lo), y: 4, z: 8, core: 2. Of those that a mesh axis runs over, the one named last changes fastest.
Arguments:
- grads: float32 [128, 4, 384, 1536], P('rep', None, 'shard'), may hold values from -6 to 6
- basis: float32 [4, 384, 128], P(None, 'shard'), may hold values from -0.3125 to 0.3125
- weights: float32 [4, 384, 1536], P(None, 'shard'), may hold values from -0.3125 to 0.3125
- first_moment: float32 [4, 128, 1536], P(None, 'shard'), may hold values from -6 to 6
- second_moment: float32 [4, 128, 1536], P(None, 'shard'), may hold values from 0.01 to 1
Outputs:
- new_weights: float32 [4, 384, 1536], P(None, 'shard')
- new_first: float32 [4, 128, 1536], P(None, 'shard')
- new_second: float32 [4, 128, 1536], P(None, 'shard')
- new_basis: float32 [4, 384, 128], P(None, 'shard')
The draws below stay inside these ranges and needn't reach their ends.
All inputs are finite; a program needn't handle non-finite values.
Results may differ from the reference program's by a relative error of at most 0.000057.
Values sent between devices are 32-bit elements; how exact they have to be, the bound alone decides.
No kernel may reach another device: no remote copies, remote signals or barrier semaphores. Data moves between devices by JAX's collectives and lax.ppermute only.
A program may use at most 128 MiB of HBM per device.

```python
import math
import jax
import jax.numpy as jnp
from jax import lax

D = 384
FF = 1536
R = 128
LAYERS = 4
ADAM_STEP = 100
REPLICAS = 128


def level_of(rng, dims, cuts, least, top_value):
    def one(position, blocks):
        draws = jax.random.uniform(jax.random.fold_in(jax.random.fold_in(rng, 6), position), (blocks,), jnp.float32, least / len(cuts), top_value / len(cuts))
        return jnp.repeat(jnp.exp(draws), dims[position] // blocks).reshape((-1,) + (1,) * (len(dims) - position - 1))

    gain = one(*cuts[0])
    for cut in cuts[1:]:
        gain = gain * one(*cut)
    return gain


def normal_values(stream_key, extent, scale, limit, pieces=(), kind=jnp.bfloat16):
    array = scale * jax.random.normal(stream_key, extent, jnp.float32)
    if pieces:
        array = array * level_of(stream_key, extent, pieces, -0.22, 0.18)
    return jnp.clip(array, -limit, limit).astype(kind)


def setup_inputs(seed: int = 0) -> dict:
    key_list = jax.random.split(jax.random.key(seed), 6)
    return {
        "grads": normal_values(key_list[0], (REPLICAS, LAYERS, D, FF), 1.0, 6.0, ((0, 128), (2, 2)), jnp.float32),
        "basis": normal_values(key_list[1], (LAYERS, D, R), D ** -0.5, 0.3125, ((1, 2),), jnp.float32),
        "weights": normal_values(key_list[2], (LAYERS, D, FF), D ** -0.5, 0.3125, ((1, 2),), jnp.float32),
        "first_moment": normal_values(key_list[3], (LAYERS, R, FF), 1.0, 6.0, ((1, 2),), jnp.float32),
        "second_moment": jnp.clip(jnp.exp(math.log(1.0) - 4.6051702 * jax.random.uniform(key_list[4], (LAYERS, R, FF), jnp.float32) ** level_of(key_list[4], (LAYERS, R, FF), ((1, 2),), -0.2, 0.2)), 0.01, 1.0),
    }


HIGH = lax.Precision.HIGHEST

def reference(grads, basis, weights, first_moment, second_moment):
    total = lax.optimization_barrier(jnp.sum(grads, axis=0))
    projected = jnp.einsum('ldr,ldf->lrf', basis, total, precision=HIGH)
    new_first = 0.9 * first_moment + 0.1 * projected
    new_second = 0.999 * second_moment + 0.001 * projected * projected
    direction = new_first / (1.0 - 0.9 ** ADAM_STEP) / (jnp.sqrt(new_second / (1.0 - 0.999 ** ADAM_STEP)) + 1e-08)
    update = jnp.einsum('ldr,lrf->ldf', basis, direction, precision=HIGH)
    new_weights = weights - 0.0125 * update
    refresh = jnp.einsum('ldf,lrf->ldr', total, projected, precision=HIGH)
    sumsq = lax.optimization_barrier(jnp.sum(refresh * refresh, axis=(1, 2)))
    factor = jnp.sqrt(jnp.float32(R)) / (2.0 * jnp.sqrt(sumsq + 1e-06))
    scaled = refresh * factor[:, None, None]
    gram = jnp.einsum('ldr,lds->lrs', scaled, scaled, precision=HIGH)
    new_basis = 1.5 * scaled - 0.5 * jnp.einsum('ldr,lrs->lds', scaled, gram, precision=HIGH)
    return (new_weights, new_first, new_second, new_basis)
```

```python
import jax
import jax.numpy as jnp
from jax import lax
from jax.sharding import Mesh, PartitionSpec as P

ADAM_STEP = 100
HIGH = lax.Precision.HIGHEST

SIZES = {"z": 8, "y": 4, "xh": 2, "core": 2, "xl": 2}
REP = ("z", "y", "xh", "core")


def shift(x, axis, k):
    n = SIZES[axis]
    return lax.ppermute(x, axis, [(i, (i + k) % n) for i in range(n)])


def flip(x, axis, bit=1):
    n = SIZES[axis]
    return lax.ppermute(x, axis, [(i, i ^ bit) for i in range(n)])


def rows(x, index, count):
    return lax.dynamic_slice_in_dim(x, index * count, count, 0)


def in_order(index, mine, other):
    first = index == 0
    return jnp.where(first, mine, other), jnp.where(first, other, mine)


def scatter_direct(x, axis):
    n, me = SIZES[axis], lax.axis_index(axis)
    count = x.shape[0] // n
    total = rows(x, me, count)
    for k in range(1, n):
        total = total + shift(rows(x, (me + k) % n, count), axis, k)
    return total


def gather_direct(x, axis):
    n, me = SIZES[axis], lax.axis_index(axis)
    count = x.shape[0]
    out = jnp.zeros((n * count,) + x.shape[1:], x.dtype)
    out = lax.dynamic_update_slice_in_dim(out, x, me * count, 0)
    for k in range(1, n):
        out = lax.dynamic_update_slice_in_dim(out, shift(x, axis, k), ((me - k) % n) * count, 0)
    return out


def scatter_exchange(x, axis):
    n = SIZES[axis]
    parts = x.reshape((n, x.shape[0] // n) + x.shape[1:])
    return jnp.sum(lax.all_to_all(parts, axis, split_axis=0, concat_axis=0), axis=0)


def on_device(grads, basis, weights, first_moment, second_moment):
    layers, depth, width = grads.shape[1:]
    rank = basis.shape[2]
    half = layers // 2
    piece = width // 64
    z, y, xh = lax.axis_index("z"), lax.axis_index("y"), lax.axis_index("xh")
    core, xl = lax.axis_index("core"), lax.axis_index("xl")
    place = (y * 2 + xh) * 8 + z

    given = flip(rows(grads[0], 1 - core, half), "core")
    pair = rows(grads[0], core, half) + given
    held = pair.reshape(half * depth, width).T
    held = scatter_direct(held, "y")
    held = scatter_direct(held, "xh")
    total = scatter_exchange(held, "z").reshape(piece, half, depth)

    basis_pair = rows(basis, core, half)
    cut = [
        jnp.swapaxes(lax.dynamic_slice(m, (core * half, 0, place * piece), (half, rank // 2, piece)), 1, 2)
        for m in (first_moment, second_moment)
    ]
    cut = jnp.concatenate(cut, axis=2)
    low, high = in_order(xl, cut, flip(cut, "xl"))
    first = jnp.concatenate([low[:, :, : rank // 2], high[:, :, : rank // 2]], axis=2)
    second = jnp.concatenate([low[:, :, rank // 2 :], high[:, :, rank // 2 :]], axis=2)

    proj = jnp.einsum("fld,ldr->lfr", total, basis_pair, precision=HIGH)
    proj = proj + flip(proj, "xl")
    new_first = 0.9 * first + 0.1 * proj
    new_second = 0.999 * second + 0.001 * proj * proj
    direction = (
        new_first
        / (1.0 - 0.9**ADAM_STEP)
        / (jnp.sqrt(new_second / (1.0 - 0.999**ADAM_STEP)) + 1e-08)
    )
    mine = jnp.where(xl == 0, proj[:, :, : rank // 2], proj[:, :, rank // 2 :])
    packed = jnp.concatenate([direction[0], direction[1], mine[0], mine[1]], axis=1)

    refresh = jnp.einsum("fld,lfr->ldr", total, proj, precision=HIGH)
    part = scatter_exchange(refresh.reshape(half * depth, rank), "z")
    part = part + flip(part, "y", 1)
    part = part + flip(part, "y", 2)
    part = part + flip(part, "xh")
    refresh = lax.all_gather(part, "z", axis=0, tiled=True).reshape(half, depth, rank)
    gram = jnp.einsum("ldr,lds->lrs", refresh, refresh, precision=HIGH)
    gram = gram + flip(gram, "xl")
    sumsq = jnp.einsum("lrr->l", gram)
    factor = jnp.sqrt(jnp.float32(rank)) / (2.0 * jnp.sqrt(sumsq + 1e-06))
    scaled = refresh * factor[:, None, None]
    gram_scaled = gram * (factor * factor)[:, None, None]
    basis_new = 1.5 * scaled - 0.5 * jnp.einsum("ldr,lrs->lds", scaled, gram_scaled, precision=HIGH)
    new_basis = jnp.concatenate(in_order(core, basis_new, flip(basis_new, "core")), axis=0)

    packed = lax.all_gather(packed, "z", axis=0, tiled=True)
    packed = gather_direct(packed, "xh")
    packed = gather_direct(packed, "y")
    packed = jnp.stack(in_order(core, packed, flip(packed, "core")))
    dirs = packed[:, :, : half * rank].reshape(2, width, half, rank)
    own = packed[:, :, half * rank :].reshape(2, width, half, rank // 2)
    own = jnp.transpose(own, (0, 2, 3, 1)).reshape(layers, rank // 2, width)
    new_first = 0.9 * first_moment + 0.1 * own
    new_second = 0.999 * second_moment + 0.001 * own * own
    dirs = jnp.transpose(dirs, (0, 2, 1, 3)).reshape(layers, width, rank)
    update = jnp.einsum("ldr,lfr->ldf", basis, dirs, precision=HIGH)
    new_weights = weights - 0.0125 * update
    return (new_weights, new_first, new_second, new_basis)


def solution(mesh):
    fine = Mesh(mesh.devices.reshape(8, 4, 2, 2, 2), ("z", "y", "xh", "core", "xl"))
    split = P(None, "xl", None)
    return jax.shard_map(
        on_device,
        mesh=fine,
        in_specs=(P(REP, None, "xl", None), split, split, split, split),
        out_specs=(split, split, split, split),
        check_vma=False,
    )
```

```python
import functools

import jax
import jax.numpy as jnp
from jax import lax
from jax.experimental import pallas as pl
from jax.experimental.pallas import tpu as pltpu
from jax.sharding import Mesh, PartitionSpec as P

ADAM_STEP = 100
HIGH = lax.Precision.HIGHEST

SIZES = {"z": 8, "y": 4, "xh": 2, "core": 2, "xl": 2}
REP = ("z", "y", "xh", "core")
ORDERS = (("y", "xh"), ("xh", "y"), ("y", "xh"))
CHUNKS = len(ORDERS)


def shift(x, axis, k):
    n = SIZES[axis]
    return lax.ppermute(x, axis, [(i, (i + k) % n) for i in range(n)])


def flip(x, axis, bit=1):
    n = SIZES[axis]
    return lax.ppermute(x, axis, [(i, i ^ bit) for i in range(n)])


def rows(x, index, count):
    return lax.dynamic_slice_in_dim(x, index * count, count, 0)


def in_order(index, mine, other):
    first = index == 0
    return jnp.where(first, mine, other), jnp.where(first, other, mine)


def after(x, *others):
    return lax.optimization_barrier((x, *others))[0]


def blocks(x, axis):
    n, me = SIZES[axis], lax.axis_index(axis)
    return [rows(x, (me + k) % n, x.shape[0] // n) for k in range(n)]


def scatter(own, sent, axis):
    for k, block in enumerate(sent, 1):
        own = own + shift(block, axis, k)
    return own


def gather(x, axis):
    n, me = SIZES[axis], lax.axis_index(axis)
    if n == 2:
        return jnp.concatenate(in_order(me, x, flip(x, axis)), axis=0)
    count = x.shape[0]
    out = jnp.zeros((n * count,) + x.shape[1:], x.dtype)
    out = lax.dynamic_update_slice_in_dim(out, x, me * count, 0)
    for k in range(1, n):
        out = lax.dynamic_update_slice_in_dim(out, shift(x, axis, k), ((me - k) % n) * count, 0)
    return out


def exchange(parts, axis):
    return lax.all_to_all(parts, axis, split_axis=0, concat_axis=0)


def copies(x, axis):
    return jnp.broadcast_to(x, (SIZES[axis],) + x.shape)


def finish_kernel(core, dir_own, dir_other, proj_own, proj_other, basis, weights, first, second, *rest):
    out_weights, out_first, out_second = rest[-3:]
    layer = pl.program_id(0)
    here = core[0] == layer // 2
    direction = jnp.where(here, dir_own[...], dir_other[...])
    update = lax.dot_general(
        basis[0], direction, (((1,), (1,)), ((), ())), precision=HIGH, preferred_element_type=jnp.float32
    )
    out_weights[0] = weights[0] - 0.0125 * update
    proj = jnp.where(here, proj_own[...], proj_other[...]).T
    half = proj.shape[0] // 2
    proj = jnp.where(layer % 2 == 0, proj[:half], proj[half:])
    out_first[0] = 0.9 * first[0] + 0.1 * proj
    out_second[0] = 0.999 * second[0] + 0.001 * proj * proj


def finish(chunk, core, own, other, basis, weights, first, second, before):
    layers, depth, width = weights.shape
    rank, some = basis.shape[2], own.shape[0]
    own_dir = pl.BlockSpec((some, rank), lambda l, c: (0, l % 2))
    own_proj = pl.BlockSpec((some, rank), lambda l, c: (0, 2))
    whole = pl.BlockSpec((1, depth, rank), lambda l, c: (l, 0, 0))
    tall = pl.BlockSpec((1, depth, some), lambda l, c: (l, 0, chunk))
    low = pl.BlockSpec((1, first.shape[1], some), lambda l, c: (l, 0, chunk))
    kept = [] if before is None else list(before)
    return pl.pallas_call(
        finish_kernel,
        grid_spec=pltpu.PrefetchScalarGridSpec(
            num_scalar_prefetch=1,
            grid=(layers,),
            in_specs=[own_dir, own_dir, own_proj, own_proj, whole, tall, low, low]
            + [pl.BlockSpec(memory_space=pl.ANY)] * len(kept),
            out_specs=[tall, low, low],
        ),
        out_shape=[jax.ShapeDtypeStruct(a.shape, a.dtype) for a in (weights, first, second)],
        input_output_aliases={9 + i: i for i in range(len(kept))},
        name="finish",
    )(core.reshape(1), own, other, own, other, basis, weights, first, second, *kept)


def on_device(grads, basis, weights, first_moment, second_moment):
    layers, depth, width = grads.shape[1:]
    rank = basis.shape[2]
    half = layers // 2
    some = width // CHUNKS
    small = some // 64
    z, y, xh = lax.axis_index("z"), lax.axis_index("y"), lax.axis_index("xh")
    core, xl = lax.axis_index("core"), lax.axis_index("xl")
    grad = grads[0]

    given = []
    for chunk in range(CHUNKS):
        if given:
            grad = after(grad, given[-1])
        given.append(lax.dynamic_slice(grad, ((1 - core) * half, 0, chunk * some), (half, depth, some)))
    grad = after(grad, given[-1])
    given = [flip(g, "core") for g in given]
    first_sent = []
    for chunk, order in enumerate(ORDERS):
        held = lax.dynamic_slice(grad, (core * half, 0, chunk * some), (half, depth, some)) + given[chunk]
        own, *sent = blocks(held.reshape(half * depth, some).T, order[0])
        grad = after(grad, *sent)
        first_sent.append((own, sent))
    last = first_sent[-1][1]
    second_sent = []
    for (own, sent), order in zip(first_sent, ORDERS):
        own, *sent = blocks(scatter(after(own, *last), sent, order[0]), order[1])
        second_sent.append((own, sent))
        last = sent
    pieces, places = [], []
    for chunk, ((own, sent), order) in enumerate(zip(second_sent, ORDERS)):
        held = scatter(after(own, *last), sent, order[1])
        pieces.append(held.reshape(SIZES["z"], small, half * depth))
        index = {"y": y, "xh": xh}
        place = (index[order[0]] * SIZES[order[1]] + index[order[1]]) * SIZES["z"] + z
        places.append(chunk * some + place * small)
    total = jnp.sum(exchange(jnp.concatenate(pieces, axis=1), "z"), axis=0)
    total = total.reshape(CHUNKS * small, half, depth)

    basis_pair = rows(basis, core, half)
    cut = []
    for moment in (first_moment, second_moment):
        mine = [lax.dynamic_slice(moment, (core * half, 0, at), (half, rank // 2, small)) for at in places]
        cut.append(jnp.swapaxes(jnp.concatenate(mine, axis=2), 1, 2))
    cut = jnp.concatenate(cut, axis=2)
    low, high = in_order(xl, cut, flip(cut, "xl"))
    first = jnp.concatenate([low[:, :, : rank // 2], high[:, :, : rank // 2]], axis=2)
    second = jnp.concatenate([low[:, :, rank // 2 :], high[:, :, rank // 2 :]], axis=2)

    proj = jnp.einsum("fld,ldr->lfr", total, basis_pair, precision=HIGH)
    proj = proj + flip(proj, "xl")
    new_first = 0.9 * first + 0.1 * proj
    new_second = 0.999 * second + 0.001 * proj * proj
    direction = (
        new_first
        / (1.0 - 0.9**ADAM_STEP)
        / (jnp.sqrt(new_second / (1.0 - 0.999**ADAM_STEP)) + 1e-08)
    )
    mine = jnp.where(xl == 0, proj[:, :, : rank // 2], proj[:, :, rank // 2 :])
    packed = jnp.stack([direction[0], direction[1], jnp.concatenate([mine[0], mine[1]], axis=1)])
    packed = packed.reshape(3 * CHUNKS * small, rank)

    refresh = jnp.einsum("fld,lfr->ldr", total, proj, precision=HIGH)
    refresh = refresh.reshape(SIZES["z"], half * depth // SIZES["z"], rank)
    both = exchange(jnp.concatenate([copies(packed, "z"), refresh], axis=1), "z")
    packed = both[:, : packed.shape[0]].reshape(SIZES["z"], 3, CHUNKS, small, rank)
    part = jnp.sum(both[:, 3 * CHUNKS * small :], axis=0)

    held = [
        jnp.concatenate([packed[:, i, chunk].reshape(SIZES["z"] * small, rank) for i in range(3)], axis=1)
        for chunk in range(CHUNKS)
    ]
    part = after(part, *held)
    wide = [gather(h, order[1]) for h, order in zip(held, ORDERS)]
    part = part + flip(part, "y", 1)
    part = after(part, wide[0], wide[2])
    part = part + flip(part, "y", 2)
    part = after(part, *wide)
    part = part + flip(part, "xh")
    ready = []
    for w, order in zip(wide, ORDERS):
        w = gather(w, order[0])
        ready.append((w, flip(w, "core")))
    done = None
    for chunk, (own, other) in enumerate(ready):
        done = finish(chunk, core, own, other, basis, weights, first_moment, second_moment, done)
    new_weights, new_first, new_second = done

    refresh = exchange(copies(part, "z"), "z").reshape(half, depth, rank)
    gram = jnp.einsum("ldr,lds->lrs", refresh, refresh, precision=HIGH)
    gram = gram + flip(gram, "xl")
    sumsq = jnp.einsum("lrr->l", gram)
    factor = jnp.sqrt(jnp.float32(rank)) / (2.0 * jnp.sqrt(sumsq + 1e-06))
    scaled = refresh * factor[:, None, None]
    gram_scaled = gram * (factor * factor)[:, None, None]
    basis_new = 1.5 * scaled - 0.5 * jnp.einsum("ldr,lrs->lds", scaled, gram_scaled, precision=HIGH)
    new_basis = jnp.concatenate(in_order(core, basis_new, flip(basis_new, "core")), axis=0)
    return (new_weights, new_first, new_second, new_basis)


def solution(mesh):
    fine = Mesh(mesh.devices.reshape(8, 4, 2, 2, 2), ("z", "y", "xh", "core", "xl"))
    split = P(None, "xl", None)
    return jax.shard_map(
        on_device,
        mesh=fine,
        in_specs=(P(REP, None, "xl", None), split, split, split, split),
        out_specs=(split, split, split, split),
        check_vma=False,
    )
```

```python
import functools

import jax
import jax.numpy as jnp
from jax import lax
from jax.experimental import pallas as pl
from jax.experimental.pallas import tpu as pltpu
from jax.sharding import Mesh, PartitionSpec as P

ADAM_STEP = 100
HIGH = lax.Precision.HIGHEST

SIZES = {"z": 8, "y": 4, "xh": 2, "core": 2, "xl": 2}
REP = ("z", "y", "xh", "core")
ORDERS = (("y", "xh"), ("xh", "y"), ("y", "xh"))
CHUNKS = len(ORDERS)


def flip(x, axis, bit=1):
    n = SIZES[axis]
    return lax.ppermute(x, axis, [(i, i ^ bit) for i in range(n)])


def rows(x, index, count):
    return lax.dynamic_slice_in_dim(x, index * count, count, 0)


def in_order(index, mine, other):
    first = index == 0
    return jnp.where(first, mine, other), jnp.where(first, other, mine)


def after(x, *others):
    return lax.optimization_barrier((x, *others))[0]


def halves(x, axis):
    n, me = SIZES[axis], lax.axis_index(axis)
    return [rows(x, (me + k) % n, x.shape[0] // n) for k in range(n)]


def gather(x, axis):
    if SIZES[axis] == 2:
        return jnp.concatenate(in_order(lax.axis_index(axis), x, flip(x, axis)), axis=0)
    return exchange(copies(x, axis), axis).reshape((-1,) + x.shape[1:])


def gather_shifts(x, axis, own):
    n, me = SIZES[axis], lax.axis_index(axis)
    out = jnp.zeros((n,) + x.shape, x.dtype)
    out = lax.dynamic_update_slice_in_dim(out, own[None], me, 0)
    for k in range(1, n):
        moved = lax.ppermute(x, axis, [(i, (i + k) % n) for i in range(n)])
        out = lax.dynamic_update_slice_in_dim(out, moved[None], (me - k) % n, 0)
    return out.reshape((-1,) + x.shape[1:])


def exchange(parts, axis):
    return lax.all_to_all(parts, axis, split_axis=0, concat_axis=0)


def copies(x, axis):
    return jnp.broadcast_to(x, (SIZES[axis],) + x.shape)


def pair_kernel(core, grad, given, out):
    both = grad[...] + given[...]
    out[...] = both.reshape(-1, both.shape[2]).T


def pair_sum(chunk, core, grad, given):
    half, depth, some = given.shape
    lanes = 256
    steps = some // lanes
    return pl.pallas_call(
        pair_kernel,
        grid_spec=pltpu.PrefetchScalarGridSpec(
            num_scalar_prefetch=1,
            grid=(steps,),
            in_specs=[
                pl.BlockSpec((half, depth, lanes), lambda i, c: (c[0], 0, chunk * steps + i)),
                pl.BlockSpec((half, depth, lanes), lambda i, c: (0, 0, i)),
            ],
            out_specs=pl.BlockSpec((lanes, half * depth), lambda i, c: (i, 0)),
        ),
        out_shape=jax.ShapeDtypeStruct((some, half * depth), grad.dtype),
        compiler_params=pltpu.CompilerParams(vmem_limit_bytes=12 << 20),
        cost_estimate=pl.CostEstimate(flops=given.size, bytes_accessed=12 * given.size, transcendentals=0),
        name="pair_sum",
    )(core.reshape(1), grad, given)


def finish_kernel(core, dir_own, dir_other, proj_own, proj_other, basis, weights, first, second, *rest):
    out_weights, out_first, out_second = rest[-3:]
    layer = pl.program_id(0)
    here = core[0] == layer // 2
    direction = jnp.where(here, dir_own[...], dir_other[...])
    update = lax.dot_general(
        basis[0], direction, (((1,), (1,)), ((), ())), precision=HIGH, preferred_element_type=jnp.float32
    )
    out_weights[0] = weights[0] - 0.0125 * update
    proj = jnp.where(here, proj_own[...], proj_other[...]).T
    half = proj.shape[0] // 2
    proj = jnp.where(layer % 2 == 0, proj[:half], proj[half:])
    out_first[0] = 0.9 * first[0] + 0.1 * proj
    out_second[0] = 0.999 * second[0] + 0.001 * proj * proj


def finish(chunk, core, own, other, basis, weights, first, second, before):
    layers, depth, width = weights.shape
    rank, some = basis.shape[2], own.shape[0]
    own_dir = pl.BlockSpec((some, rank), lambda l, c: (0, l % 2))
    own_proj = pl.BlockSpec((some, rank), lambda l, c: (0, 2))
    whole = pl.BlockSpec((1, depth, rank), lambda l, c: (l, 0, 0))
    tall = pl.BlockSpec((1, depth, some), lambda l, c: (l, 0, chunk))
    low = pl.BlockSpec((1, first.shape[1], some), lambda l, c: (l, 0, chunk))
    kept = [] if before is None else list(before)
    return pl.pallas_call(
        finish_kernel,
        grid_spec=pltpu.PrefetchScalarGridSpec(
            num_scalar_prefetch=1,
            grid=(layers,),
            in_specs=[own_dir, own_dir, own_proj, own_proj, whole, tall, low, low]
            + [pl.BlockSpec(memory_space=pl.ANY)] * len(kept),
            out_specs=[tall, low, low],
        ),
        out_shape=[jax.ShapeDtypeStruct(a.shape, a.dtype) for a in (weights, first, second)],
        input_output_aliases={9 + i: i for i in range(len(kept))},
        compiler_params=pltpu.CompilerParams(vmem_limit_bytes=12 << 20),
        cost_estimate=pl.CostEstimate(
            flops=12 * layers * depth * rank * some, bytes_accessed=8 * layers * (depth + rank) * some, transcendentals=0
        ),
        name="finish",
    )(core.reshape(1), own, other, own, other, basis, weights, first, second, *kept)


def on_device(grads, basis, weights, first_moment, second_moment):
    layers, depth, width = grads.shape[1:]
    rank = basis.shape[2]
    half = layers // 2
    some = width // CHUNKS
    small = some // 64
    z, y, xh = lax.axis_index("z"), lax.axis_index("y"), lax.axis_index("xh")
    core, xl = lax.axis_index("core"), lax.axis_index("xl")
    grad = grads[0]
    kept = [pltpu.with_memory_space_constraint(a, pltpu.HBM) for a in (grad, weights, first_moment, second_moment)]

    given = []
    for chunk in range(CHUNKS):
        if given:
            grad = after(grad, given[-1])
        given.append(lax.dynamic_slice(grad, ((1 - core) * half, 0, chunk * some), (half, depth, some)))
    given = [flip(g, "core") for g in given]
    held = [pair_sum(chunk, core, kept[0], given[chunk]) for chunk in range(CHUNKS)]
    by_y = lambda x: jnp.sum(exchange(x.reshape((SIZES["y"], -1) + x.shape[1:]), "y"), axis=0)
    own, sent = halves(held[1], "xh")
    held[0] = by_y(held[0])
    held[2] = by_y(held[2])
    held[1] = by_y(own + flip(sent, "xh"))
    for chunk in (0, 2):
        own, sent = halves(held[chunk], "xh")
        held[chunk] = own + flip(sent, "xh")
    pieces, places = [], []
    for chunk, order in enumerate(ORDERS):
        pieces.append(held[chunk].reshape(SIZES["z"], small, half * depth))
        index = {"y": y, "xh": xh}
        place = (index[order[0]] * SIZES[order[1]] + index[order[1]]) * SIZES["z"] + z
        places.append(chunk * some + place * small)
    total = jnp.sum(exchange(jnp.concatenate(pieces, axis=1), "z"), axis=0)
    total = total.reshape(CHUNKS * small, half, depth)

    basis_pair = rows(basis, core, half)
    cut = []
    for moment in (first_moment, second_moment):
        mine = [lax.dynamic_slice(moment, (core * half, 0, at), (half, rank // 2, small)) for at in places]
        cut.append(jnp.swapaxes(jnp.concatenate(mine, axis=2), 1, 2))
    cut = jnp.concatenate(cut, axis=2)
    low, high = in_order(xl, cut, flip(cut, "xl"))
    first = jnp.concatenate([low[:, :, : rank // 2], high[:, :, : rank // 2]], axis=2)
    second = jnp.concatenate([low[:, :, rank // 2 :], high[:, :, rank // 2 :]], axis=2)

    proj = jnp.einsum("fld,ldr->lfr", total, basis_pair, precision=HIGH)
    proj = proj + flip(proj, "xl")
    new_first = 0.9 * first + 0.1 * proj
    new_second = 0.999 * second + 0.001 * proj * proj
    direction = (
        new_first
        / (1.0 - 0.9**ADAM_STEP)
        / (jnp.sqrt(new_second / (1.0 - 0.999**ADAM_STEP)) + 1e-08)
    )
    mine = jnp.where(xl == 0, proj[:, :, : rank // 2], proj[:, :, rank // 2 :])
    packed = jnp.stack([direction[0], direction[1], jnp.concatenate([mine[0], mine[1]], axis=1)])
    packed = packed.reshape(3 * CHUNKS * small, rank)

    refresh = jnp.einsum("fld,lfr->ldr", total, proj, precision=HIGH)
    refresh = refresh.reshape(SIZES["z"], half * depth // SIZES["z"], rank)
    both = exchange(jnp.concatenate([copies(packed, "z"), refresh], axis=1), "z")
    packed = both[:, : packed.shape[0]].reshape(SIZES["z"], 3, CHUNKS, small, rank)
    part = jnp.sum(both[:, 3 * CHUNKS * small :], axis=0)

    held = [
        jnp.concatenate([packed[:, i, chunk].reshape(SIZES["z"] * small, rank) for i in range(3)], axis=1)
        for chunk in range(CHUNKS)
    ]
    count = held[1].shape[0]
    extra = part.reshape(-1, half * depth)
    both = exchange(copies(jnp.concatenate([held[1], extra]), "y"), "y")
    middle = both[:, :count].reshape(SIZES["y"] * count, half * depth)
    part = jnp.sum(both[:, count:], axis=0).reshape(part.shape)
    part = part + flip(part, "xh")
    sides = [gather(held[chunk], "xh") for chunk in (0, 2)]
    wide = [gather(sides[0], "y"), gather(middle, "xh")]
    done = None
    for chunk in range(CHUNKS):
        if chunk == 2:
            moved = after(sides[1], wide[0])
            wide.append(gather_shifts(moved, "y", after(moved, *done)))
        other = flip(wide[chunk], "core")
        done = finish(chunk, core, wide[chunk], other, basis, *kept[1:], done)
    new_weights, new_first, new_second = done

    refresh = exchange(copies(part, "z"), "z").reshape(half, depth, rank)
    gram = jnp.einsum("ldr,lds->lrs", refresh, refresh, precision=HIGH)
    gram = gram + flip(gram, "xl")
    sumsq = jnp.einsum("lrr->l", gram)
    factor = jnp.sqrt(jnp.float32(rank)) / (2.0 * jnp.sqrt(sumsq + 1e-06))
    scaled = refresh * factor[:, None, None]
    gram_scaled = gram * (factor * factor)[:, None, None]
    basis_new = 1.5 * scaled - 0.5 * jnp.einsum("ldr,lrs->lds", scaled, gram_scaled, precision=HIGH)
    new_basis = jnp.concatenate(in_order(core, basis_new, flip(basis_new, "core")), axis=0)
    return (new_weights, new_first, new_second, new_basis)


def solution(mesh):
    fine = Mesh(mesh.devices.reshape(8, 4, 2, 2, 2), ("z", "y", "xh", "core", "xl"))
    split = P(None, "xl", None)
    return jax.shard_map(
        on_device,
        mesh=fine,
        in_specs=(P(REP, None, "xl", None), split, split, split, split),
        out_specs=(split, split, split, split),
        check_vma=False,
    )
```

```python
import jax
import jax.numpy as jnp
from jax import lax
from jax.experimental import pallas as pl
from jax.experimental.pallas import tpu as pltpu
from jax.sharding import Mesh, PartitionSpec as P

ADAM_STEP = 100
HIGH = lax.Precision.HIGHEST

SIZES = {"z": 8, "y": 4, "xh": 2, "core": 2, "xl": 2}
REP = ("z", "y", "xh", "core")
ORDERS = (("y", "xh"), ("xh", "y"), ("y", "xh"))
CHUNKS = len(ORDERS)
TOGETHER = (0, 2, 1)


def flip(x, axis, bit=1):
    n = SIZES[axis]
    return lax.ppermute(x, axis, [(i, i ^ bit) for i in range(n)])


def rows(x, index, count):
    return lax.dynamic_slice_in_dim(x, index * count, count, 0)


def in_order(index, mine, other):
    first = index == 0
    return jnp.where(first, mine, other), jnp.where(first, other, mine)


def after(x, *others):
    return lax.optimization_barrier((x, *others))[0]


def scatter(parts, axis):
    n = SIZES[axis]
    total = parts[0]
    for k in range(1, n):
        total = total + lax.ppermute(parts[k], axis, [(i, (i + k) % n) for i in range(n)])
    return total


def blocks(x, axis):
    n, me = SIZES[axis], lax.axis_index(axis)
    return [rows(x, (me + k) % n, x.shape[0] // n) for k in range(n)]


def gather(x, axis, own=None):
    n, me = SIZES[axis], lax.axis_index(axis)
    own = x if own is None else own
    if n == 2:
        return jnp.stack(in_order(me, own, flip(x, axis)))
    return settle(own, around(x, axis), axis)


def around(x, axis):
    n = SIZES[axis]
    return [lax.ppermute(x, axis, [(i, (i + k) % n) for i in range(n)]) for k in range(1, n)]


def settle(own, moved, axis):
    n, me = SIZES[axis], lax.axis_index(axis)
    out = jnp.zeros((n,) + own.shape, own.dtype)
    for k, block in enumerate([own] + moved):
        out = lax.dynamic_update_slice_in_dim(out, block[None], (me - k) % n, 0)
    return out


def exchange(parts, axis):
    return lax.all_to_all(parts, axis, split_axis=0, concat_axis=0)


def copies(x, axis):
    return jnp.broadcast_to(x, (SIZES[axis],) + x.shape)


def pair_kernel(where, grad, given, *outs):
    step = pl.program_id(0)
    both = grad[...] + given[...]
    both = both.reshape(-1, both.shape[2]).T
    for k, out in enumerate(outs):

        @pl.when(step == k)
        def _():
            out[...] = both


def pair_sum(chunk, core, axis, grad, given):
    half, depth, some = given.shape
    n = SIZES[axis]
    lanes = some // n
    out = jax.ShapeDtypeStruct((lanes, half * depth), grad.dtype)
    return pl.pallas_call(
        pair_kernel,
        grid_spec=pltpu.PrefetchScalarGridSpec(
            num_scalar_prefetch=1,
            grid=(n,),
            in_specs=[
                pl.BlockSpec((half, depth, lanes), lambda k, w: (w[0], 0, chunk * n + (w[1] + k) % n)),
                pl.BlockSpec((half, depth, lanes), lambda k, w: (0, 0, (w[1] + k) % n)),
            ],
            out_specs=[pl.BlockSpec(out.shape, lambda k, w: (0, 0))] * n,
        ),
        out_shape=[out] * n,
        compiler_params=pltpu.CompilerParams(vmem_limit_bytes=12 << 20),
        cost_estimate=pl.CostEstimate(flops=given.size, bytes_accessed=12 * given.size, transcendentals=0),
        name="pair_sum",
    )(jnp.stack([core, lax.axis_index(axis)]), grad, given)


def finish_kernel(core, own, other, basis, weights, first, second, *rest):
    out_weights, out_first, out_second = rest[-3:]
    layer = pl.program_id(1)
    rank = basis.shape[2]
    here = core[0] == layer // 2
    some = out_weights.shape[2]
    x = jnp.where(here, own[...].reshape(some, -1), other[...].reshape(some, -1))
    direction = jnp.where(layer % 2 == 0, x[:, :rank], x[:, rank : 2 * rank])
    update = lax.dot_general(
        basis[0], direction, (((1,), (1,)), ((), ())), precision=HIGH, preferred_element_type=jnp.float32
    )
    out_weights[0] = weights[0] - 0.0125 * update
    proj = x[:, 2 * rank :].T
    proj = jnp.where(layer % 2 == 0, proj[: rank // 2], proj[rank // 2 :])
    out_first[0] = 0.9 * first[0] + 0.1 * proj
    out_second[0] = 0.999 * second[0] + 0.001 * proj * proj


def finish(chunks, core, own, other, basis, weights, first, second, before):
    layers, depth, width = weights.shape
    rank, some = basis.shape[2], width // CHUNKS
    gap = chunks[-1] - chunks[0]
    small = own.shape[2]
    packed = pl.BlockSpec((own.shape[0], 1, small, own.shape[3]), lambda h, l, c: (0, h, 0, 0))
    whole = pl.BlockSpec((1, depth, rank), lambda h, l, c: (l, 0, 0))
    tall = pl.BlockSpec((1, depth, some), lambda h, l, c: (l, 0, chunks[0] + gap * h))
    low = pl.BlockSpec((1, first.shape[1], some), lambda h, l, c: (l, 0, chunks[0] + gap * h))
    kept = [] if before is None else list(before)
    return pl.pallas_call(
        finish_kernel,
        grid_spec=pltpu.PrefetchScalarGridSpec(
            num_scalar_prefetch=1,
            grid=(len(chunks), layers),
            in_specs=[packed, packed, whole, tall, low, low] + [pl.BlockSpec(memory_space=pl.ANY)] * len(kept),
            out_specs=[tall, low, low],
        ),
        out_shape=[jax.ShapeDtypeStruct(a.shape, a.dtype) for a in (weights, first, second)],
        input_output_aliases={7 + i: i for i in range(len(kept))},
        compiler_params=pltpu.CompilerParams(vmem_limit_bytes=20 << 20),
        cost_estimate=pl.CostEstimate(
            flops=12 * layers * depth * rank * some * len(chunks),
            bytes_accessed=8 * layers * (depth + rank) * some * len(chunks),
            transcendentals=0,
        ),
        name="finish",
    )(core.reshape(1), own, other, basis, weights, first, second, *kept)


def on_device(grads, basis, weights, first_moment, second_moment):
    layers, depth, width = grads.shape[1:]
    rank = basis.shape[2]
    half = layers // 2
    some = width // CHUNKS
    small = some // 64
    z, y, xh = lax.axis_index("z"), lax.axis_index("y"), lax.axis_index("xh")
    core, xl = lax.axis_index("core"), lax.axis_index("xl")
    grad = grads[0]
    kept = pltpu.with_memory_space_constraint(grad, pltpu.HBM)

    given = []
    for chunk in range(CHUNKS):
        if given:
            grad = after(grad, given[-1])
        given.append(lax.dynamic_slice(grad, ((1 - core) * half, 0, chunk * some), (half, depth, some)))
    given = [flip(g, "core") for g in given]
    sent = [list(pair_sum(chunk, core, order[0], kept, given[chunk])) for chunk, order in enumerate(ORDERS)]
    last = sent[-1]
    nearby = [pltpu.with_memory_space_constraint(a, pltpu.HBM) for a in (weights, first_moment, second_moment)]
    for stage in (0, 1):
        sums = []
        for parts, order in zip(sent, ORDERS):
            summed = scatter([after(parts[0], *last)] + parts[1:], order[stage])
            if stage == 0:
                summed = blocks(summed, order[1])
                last = summed
            sums.append(summed)
        sent = sums
    pieces, places = [], []
    for chunk in TOGETHER:
        order = ORDERS[chunk]
        pieces.append(sent[chunk].reshape(SIZES["z"], small, half * depth))
        index = {"y": y, "xh": xh}
        place = (index[order[0]] * SIZES[order[1]] + index[order[1]]) * SIZES["z"] + z
        places.append(chunk * some + place * small)
    total = jnp.sum(exchange(jnp.concatenate(pieces, axis=1), "z"), axis=0)
    total = total.reshape(CHUNKS * small, half, depth)

    basis_pair = rows(basis, core, half)
    cut = []
    for moment in (first_moment, second_moment):
        mine = [lax.dynamic_slice(moment, (core * half, 0, at), (half, rank // 2, small)) for at in places]
        cut.append(jnp.swapaxes(jnp.concatenate(mine, axis=2), 1, 2))
    cut = jnp.concatenate(cut, axis=2)
    low, high = in_order(xl, cut, flip(cut, "xl"))
    first = jnp.concatenate([low[:, :, : rank // 2], high[:, :, : rank // 2]], axis=2)
    second = jnp.concatenate([low[:, :, rank // 2 :], high[:, :, rank // 2 :]], axis=2)

    proj = jnp.einsum("fld,ldr->lfr", total, basis_pair, precision=HIGH)
    proj = proj + flip(proj, "xl")
    new_first = 0.9 * first + 0.1 * proj
    new_second = 0.999 * second + 0.001 * proj * proj
    direction = (
        new_first
        / (1.0 - 0.9**ADAM_STEP)
        / (jnp.sqrt(new_second / (1.0 - 0.999**ADAM_STEP)) + 1e-08)
    )
    mine = jnp.where(xl == 0, proj[:, :, : rank // 2], proj[:, :, rank // 2 :])
    packed = jnp.concatenate([direction[0], direction[1], mine[0], mine[1]], axis=1)

    refresh = jnp.einsum("fld,lfr->ldr", total, proj, precision=HIGH)
    refresh = refresh.reshape(SIZES["z"], 3, -1, rank)
    refresh = jnp.concatenate([refresh[:, i] for i in range(3)], axis=2)
    both = exchange(jnp.concatenate([copies(packed, "z"), refresh], axis=1), "z")
    large = both[:, : 2 * small].reshape(-1, 3 * rank)
    little = both[:, 2 * small : 3 * small].reshape(-1, 3 * rank)
    part = jnp.sum(both[:, 3 * small :], axis=0)

    little = jnp.concatenate([little, part])
    large = gather(large, "xh").reshape(-1, 3 * rank)
    moved = around(large, "y")
    little = settle(after(little, large), around(little, "y"), "y")
    part = jnp.sum(little[:, -part.shape[0] :], axis=0)
    little = little[:, : -part.shape[0]].reshape(-1, 3 * rank)
    part = part + flip(part, "xh")
    large = settle(large, moved, "y").reshape(-1, 2, small, 3 * rank)
    little = gather(little, "xh", after(little, large)).reshape(-1, 1, small, 3 * rank)
    done = finish((0, 2), core, large, flip(large, "core"), basis, *nearby, None)
    done = finish((1,), core, little, flip(little, "core"), basis, *nearby, done)
    new_weights, new_first, new_second = done

    refresh = after(exchange(copies(part, "z"), "z"), large)
    refresh = jnp.stack([refresh[:, :, i * rank : (i + 1) * rank] for i in range(3)], axis=1)
    refresh = refresh.reshape(half, depth, rank)
    gram = jnp.einsum("ldr,lds->lrs", refresh, refresh, precision=HIGH)
    gram = gram + flip(gram, "xl")
    sumsq = jnp.einsum("lrr->l", gram)
    factor = jnp.sqrt(jnp.float32(rank)) / (2.0 * jnp.sqrt(sumsq + 1e-06))
    scaled = refresh * factor[:, None, None]
    gram_scaled = gram * (factor * factor)[:, None, None]
    basis_new = 1.5 * scaled - 0.5 * jnp.einsum("ldr,lrs->lds", scaled, gram_scaled, precision=HIGH)
    new_basis = jnp.concatenate(in_order(core, basis_new, flip(basis_new, "core")), axis=0)
    return (new_weights, new_first, new_second, new_basis)


def solution(mesh):
    fine = Mesh(mesh.devices.reshape(8, 4, 2, 2, 2), ("z", "y", "xh", "core", "xl"))
    split = P(None, "xl", None)
    return jax.shard_map(
        on_device,
        mesh=fine,
        in_specs=(P(REP, None, "xl", None), split, split, split, split),
        out_specs=(split, split, split, split),
        check_vma=False,
    )
```

```python
import jax
import jax.numpy as jnp
from jax import lax
from jax.experimental import pallas as pl
from jax.experimental.pallas import tpu as pltpu
from jax.sharding import Mesh, PartitionSpec as P

ADAM_STEP = 100
HIGH = lax.Precision.HIGHEST

SIZES = {"z": 8, "y": 4, "xh": 2, "core": 2, "xl": 2}
REP = ("z", "y", "xh", "core")
ORDERS = (("y", "xh"), ("xh", "y"), ("y", "xh"))
CHUNKS = len(ORDERS)
TOGETHER = (0, 2, 1)


def flip(x, axis, bit=1):
    n = SIZES[axis]
    return lax.ppermute(x, axis, [(i, i ^ bit) for i in range(n)])


def rows(x, index, count):
    return lax.dynamic_slice_in_dim(x, index * count, count, 0)


def in_order(index, mine, other):
    first = index == 0
    return jnp.where(first, mine, other), jnp.where(first, other, mine)


def after(x, *others):
    return lax.optimization_barrier((x, *others))[0]


def scatter(parts, axis):
    n = SIZES[axis]
    total = parts[0]
    for k in range(1, n):
        total = total + lax.ppermute(parts[k], axis, [(i, (i + k) % n) for i in range(n)])
    return total


def blocks(x, axis):
    n, me = SIZES[axis], lax.axis_index(axis)
    return [rows(x, (me + k) % n, x.shape[0] // n) for k in range(n)]


def gather(x, axis, own=None):
    n, me = SIZES[axis], lax.axis_index(axis)
    own = x if own is None else own
    if n == 2:
        return jnp.stack(in_order(me, own, flip(x, axis)))
    return settle(own, around(x, axis), axis)


def around(x, axis):
    n = SIZES[axis]
    return [lax.ppermute(x, axis, [(i, (i + k) % n) for i in range(n)]) for k in range(1, n)]


def settle(own, moved, axis):
    n, me = SIZES[axis], lax.axis_index(axis)
    out = jnp.zeros((n,) + own.shape, own.dtype)
    for k, block in enumerate([own] + moved):
        out = lax.dynamic_update_slice_in_dim(out, block[None], (me - k) % n, 0)
    return out


def exchange(parts, axis):
    return lax.all_to_all(parts, axis, split_axis=0, concat_axis=0)


def copies(x, axis):
    return jnp.broadcast_to(x, (SIZES[axis],) + x.shape)


def finish_kernel(core, own, other, basis, weights, first, second, *rest):
    out_weights, out_first, out_second = rest[-3:]
    layer = pl.program_id(1)
    rank = basis.shape[2]
    here = core[0] == layer // 2
    some = out_weights.shape[2]
    x = jnp.where(here, own[...].reshape(some, -1), other[...].reshape(some, -1))
    direction = jnp.where(layer % 2 == 0, x[:, :rank], x[:, rank : 2 * rank])
    update = lax.dot_general(
        basis[0], direction, (((1,), (1,)), ((), ())), precision=HIGH, preferred_element_type=jnp.float32
    )
    out_weights[0] = weights[0] - 0.0125 * update
    proj = x[:, 2 * rank :].T
    proj = jnp.where(layer % 2 == 0, proj[: rank // 2], proj[rank // 2 :])
    out_first[0] = 0.9 * first[0] + 0.1 * proj
    out_second[0] = 0.999 * second[0] + 0.001 * proj * proj


def finish(chunks, core, own, other, basis, weights, first, second, before):
    layers, depth, width = weights.shape
    rank, some = basis.shape[2], width // CHUNKS
    gap = chunks[-1] - chunks[0]
    small = own.shape[2]
    packed = pl.BlockSpec((own.shape[0], 1, small, own.shape[3]), lambda h, l, c: (0, h, 0, 0))
    whole = pl.BlockSpec((1, depth, rank), lambda h, l, c: (l, 0, 0))
    tall = pl.BlockSpec((1, depth, some), lambda h, l, c: (l, 0, chunks[0] + gap * h))
    low = pl.BlockSpec((1, first.shape[1], some), lambda h, l, c: (l, 0, chunks[0] + gap * h))
    kept = [] if before is None else list(before)
    return pl.pallas_call(
        finish_kernel,
        grid_spec=pltpu.PrefetchScalarGridSpec(
            num_scalar_prefetch=1,
            grid=(len(chunks), layers),
            in_specs=[packed, packed, whole, tall, low, low] + [pl.BlockSpec(memory_space=pl.ANY)] * len(kept),
            out_specs=[tall, low, low],
        ),
        out_shape=[jax.ShapeDtypeStruct(a.shape, a.dtype) for a in (weights, first, second)],
        input_output_aliases={7 + i: i for i in range(len(kept))},
        compiler_params=pltpu.CompilerParams(vmem_limit_bytes=20 << 20),
        cost_estimate=pl.CostEstimate(
            flops=12 * layers * depth * rank * some * len(chunks),
            bytes_accessed=8 * layers * (depth + rank) * some * len(chunks),
            transcendentals=0,
        ),
        name="finish",
    )(core.reshape(1), own, other, basis, weights, first, second, *kept)


def on_device(grads, basis, weights, first_moment, second_moment):
    layers, depth, width = grads.shape[1:]
    rank = basis.shape[2]
    half = layers // 2
    some = width // CHUNKS
    small = some // 64
    z, y, xh = lax.axis_index("z"), lax.axis_index("y"), lax.axis_index("xh")
    core, xl = lax.axis_index("core"), lax.axis_index("xl")
    grad = grads[0]

    given, sent = [], []
    for step, chunk in (("give", 0), ("give", 1), ("add", 0), ("give", 2), ("add", 1), ("add", 2)):
        if step == "give":
            part = lax.dynamic_slice(grad, ((1 - core) * half, 0, chunk * some), (half, depth, some))
            grad = after(grad, part)
            given.append(flip(part, "core"))
        else:
            pair = lax.dynamic_slice(grad, (core * half, 0, chunk * some), (half, depth, some)) + given[chunk]
            sent.append(blocks(pair.reshape(half * depth, some).T, ORDERS[chunk][0]))
            grad = after(grad, *sent[-1])
    last = sent[-1]
    nearby = [pltpu.with_memory_space_constraint(a, pltpu.HBM) for a in (weights, first_moment, second_moment)]
    early = last
    for stage in (0, 1):
        sums = []
        for parts, order in zip(sent, ORDERS):
            summed = scatter([after(parts[0], *last)] + parts[1:], order[stage])
            if stage == 0:
                summed = blocks(summed, order[1])
                last = summed
            sums.append(summed)
        sent = sums
    pieces, places = [], []
    for chunk in TOGETHER:
        order = ORDERS[chunk]
        pieces.append(sent[chunk].reshape(SIZES["z"], small, half * depth))
        index = {"y": y, "xh": xh}
        place = (index[order[0]] * SIZES[order[1]] + index[order[1]]) * SIZES["z"] + z
        places.append(after(chunk * some + place * small, *early))
    total = jnp.sum(exchange(jnp.concatenate(pieces, axis=1), "z"), axis=0)
    total = total.reshape(CHUNKS * small, half, depth)

    basis_pair = rows(basis, core, half)
    cut = []
    for moment in (first_moment, second_moment):
        mine = [lax.dynamic_slice(moment, (core * half, 0, at), (half, rank // 2, small)) for at in places]
        cut.append(jnp.swapaxes(jnp.concatenate(mine, axis=2), 1, 2))
    cut = jnp.concatenate(cut, axis=2)
    low, high = in_order(xl, cut, flip(cut, "xl"))
    first = jnp.concatenate([low[:, :, : rank // 2], high[:, :, : rank // 2]], axis=2)
    second = jnp.concatenate([low[:, :, rank // 2 :], high[:, :, rank // 2 :]], axis=2)

    proj = jnp.einsum("fld,ldr->lfr", total, basis_pair, precision=HIGH)
    proj = proj + flip(proj, "xl")
    new_first = 0.9 * first + 0.1 * proj
    new_second = 0.999 * second + 0.001 * proj * proj
    direction = (
        new_first
        / (1.0 - 0.9**ADAM_STEP)
        / (jnp.sqrt(new_second / (1.0 - 0.999**ADAM_STEP)) + 1e-08)
    )
    mine = jnp.where(xl == 0, proj[:, :, : rank // 2], proj[:, :, rank // 2 :])
    packed = jnp.concatenate([direction[0], direction[1], mine[0], mine[1]], axis=1)

    refresh = jnp.einsum("fld,lfr->ldr", total, proj, precision=HIGH)
    refresh = refresh.reshape(SIZES["z"], 3, -1, rank)
    refresh = jnp.concatenate([refresh[:, i] for i in range(3)], axis=2)
    both = exchange(jnp.concatenate([copies(packed, "z"), refresh], axis=1), "z")
    large = both[:, : 2 * small].reshape(-1, 3 * rank)
    little = both[:, 2 * small : 3 * small].reshape(-1, 3 * rank)
    part = jnp.sum(both[:, 3 * small :], axis=0)

    little = jnp.concatenate([little, part])
    large = gather(large, "xh").reshape(-1, 3 * rank)
    small_y = around(little, "y")
    across = exchange(copies(large, "y"), "y").reshape(-1, 2, small, 3 * rank)
    little = settle(after(little, large), small_y, "y")
    part = jnp.sum(little[:, -part.shape[0] :], axis=0)
    little = little[:, : -part.shape[0]].reshape(-1, 3 * rank)
    part = part + flip(part, "xh")
    little = gather(little, "xh", after(little, across)).reshape(-1, 1, small, 3 * rank)

    refresh = part
    for bit in range(3):
        if bit == 2:
            refresh = after(refresh, across)
        refresh = jnp.concatenate(in_order((z >> bit) & 1, refresh, flip(refresh, "z", 1 << bit)))
    refresh = refresh.reshape(SIZES["z"], -1, 3 * rank)
    refresh = jnp.stack([refresh[:, :, i * rank : (i + 1) * rank] for i in range(3)], axis=1)
    refresh = refresh.reshape(half, depth, rank)
    gram = jnp.einsum("ldr,lds->lrs", refresh, refresh, precision=HIGH)

    other = flip(across, "core")
    first_done = finish((0, 2), core, after(across, gram), other, basis, *nearby, None)
    done = finish((1,), core, little, flip(little, "core"), basis, *nearby, first_done)
    new_weights, new_first, new_second = done
    gram = after(gram, *first_done) + flip(gram, "xl")
    sumsq = jnp.einsum("lrr->l", gram)
    factor = jnp.sqrt(jnp.float32(rank)) / (2.0 * jnp.sqrt(sumsq + 1e-06))
    scaled = refresh * factor[:, None, None]
    gram_scaled = gram * (factor * factor)[:, None, None]
    basis_new = 1.5 * scaled - 0.5 * jnp.einsum("ldr,lrs->lds", scaled, gram_scaled, precision=HIGH)
    new_basis = jnp.concatenate(in_order(core, after(basis_new, *done), flip(basis_new, "core")), axis=0)
    return (new_weights, new_first, new_second, new_basis)


def solution(mesh):
    fine = Mesh(mesh.devices.reshape(8, 4, 2, 2, 2), ("z", "y", "xh", "core", "xl"))
    split = P(None, "xl", None)
    return jax.shard_map(
        on_device,
        mesh=fine,
        in_specs=(P(REP, None, "xl", None), split, split, split, split),
        out_specs=(split, split, split, split),
        check_vma=False,
    )
```

```python
import functools

import jax
import jax.numpy as jnp
from jax import lax
from jax.experimental import pallas as pl
from jax.experimental.pallas import tpu as pltpu
from jax.sharding import Mesh, PartitionSpec as P

ADAM_STEP = 100
HIGH = lax.Precision.HIGHEST

SIZES = {"z": 8, "y": 4, "xh": 2, "core": 2, "xl": 2}
REP = ("z", "y", "xh", "core")
ORDERS = (("y", "xh"), ("xh", "y"), ("y", "xh"))
CHUNKS = len(ORDERS)
TOGETHER = (0, 2, 1)


def flip(x, axis, bit=1):
    n = SIZES[axis]
    return lax.ppermute(x, axis, [(i, i ^ bit) for i in range(n)])


def rows(x, index, count):
    return lax.dynamic_slice_in_dim(x, index * count, count, 0)


def in_order(index, mine, other):
    first = index == 0
    return jnp.where(first, mine, other), jnp.where(first, other, mine)


def after(x, *others):
    return lax.optimization_barrier((x, *others))[0]


def scatter(parts, axis):
    n = SIZES[axis]
    total = parts[0]
    for k in range(1, n):
        total = total + lax.ppermute(parts[k], axis, [(i, (i + k) % n) for i in range(n)])
    return total


def blocks(x, axis):
    n, me = SIZES[axis], lax.axis_index(axis)
    return [rows(x, (me + k) % n, x.shape[0] // n) for k in range(n)]


def gather(x, axis, own=None):
    n, me = SIZES[axis], lax.axis_index(axis)
    own = x if own is None else own
    if n == 2:
        return jnp.stack(in_order(me, own, flip(x, axis)))
    return settle(own, around(x, axis), axis)


def around(x, axis):
    n = SIZES[axis]
    return [lax.ppermute(x, axis, [(i, (i + k) % n) for i in range(n)]) for k in range(1, n)]


def settle(own, moved, axis):
    n, me = SIZES[axis], lax.axis_index(axis)
    out = jnp.zeros((n,) + own.shape, own.dtype)
    for k, block in enumerate([own] + moved):
        out = lax.dynamic_update_slice_in_dim(out, block[None], (me - k) % n, 0)
    return out


def exchange(parts, axis):
    return lax.all_to_all(parts, axis, split_axis=0, concat_axis=0)


def copies(x, axis):
    return jnp.broadcast_to(x, (SIZES[axis],) + x.shape)


def finish_kernel(count, *refs):
    sources = refs[1 : 1 + count]
    basis, weights, first, second = refs[1 + count : 5 + count]
    out_weights, out_first, out_second = refs[-3:]
    rank = basis.shape[2]
    some = out_weights.shape[2]
    step = pl.program_id(1)
    sources = [source[...].reshape(some, -1) for source in sources]
    x = sources[0] if count == 1 else jnp.where(step < 2, *sources)
    direction = jnp.where(step % 2 == 0, x[:, :rank], x[:, rank : 2 * rank])
    update = lax.dot_general(
        basis[0], direction, (((1,), (1,)), ((), ())), precision=HIGH, preferred_element_type=jnp.float32
    )
    out_weights[0] = weights[0] - 0.0125 * update
    proj = x[:, 2 * rank :].T
    proj = jnp.where(step % 2 == 0, proj[: rank // 2], proj[rank // 2 :])
    out_first[0] = 0.9 * first[0] + 0.1 * proj
    out_second[0] = 0.999 * second[0] + 0.001 * proj * proj


def finish(chunks, pairs, sources, basis, weights, first, second, before):
    layers, depth, width = weights.shape
    rank, some = basis.shape[2], width // CHUNKS
    gap = chunks[-1] - chunks[0]
    shape = sources[0].shape
    layer = lambda j, p: p[j // 2] * 2 + j % 2
    packed = pl.BlockSpec((shape[0], 1) + shape[2:], lambda h, j, p: (0, h, 0, 0))
    whole = pl.BlockSpec((1, depth, rank), lambda h, j, p: (layer(j, p), 0, 0))
    tall = pl.BlockSpec((1, depth, some), lambda h, j, p: (layer(j, p), 0, chunks[0] + gap * h))
    low = pl.BlockSpec((1, first.shape[1], some), lambda h, j, p: (layer(j, p), 0, chunks[0] + gap * h))
    kept = [] if before is None else list(before)
    count = len(sources)
    steps = 2 * count
    return pl.pallas_call(
        functools.partial(finish_kernel, count),
        grid_spec=pltpu.PrefetchScalarGridSpec(
            num_scalar_prefetch=1,
            grid=(len(chunks), steps),
            in_specs=[packed] * count + [whole, tall, low, low] + [pl.BlockSpec(memory_space=pl.ANY)] * len(kept),
            out_specs=[tall, low, low],
        ),
        out_shape=[jax.ShapeDtypeStruct(a.shape, a.dtype) for a in (weights, first, second)],
        input_output_aliases={5 + count + i: i for i in range(len(kept))},
        compiler_params=pltpu.CompilerParams(vmem_limit_bytes=20 << 20),
        cost_estimate=pl.CostEstimate(
            flops=12 * steps * depth * rank * some * len(chunks),
            bytes_accessed=8 * steps * (depth + rank) * some * len(chunks),
            transcendentals=0,
        ),
        name="finish",
    )(jnp.stack(pairs), *sources, basis, weights, first, second, *kept)


def on_device(grads, basis, weights, first_moment, second_moment):
    layers, depth, width = grads.shape[1:]
    rank = basis.shape[2]
    half = layers // 2
    some = width // CHUNKS
    small = some // 64
    z, y, xh = lax.axis_index("z"), lax.axis_index("y"), lax.axis_index("xh")
    core, xl = lax.axis_index("core"), lax.axis_index("xl")
    grad = grads[0]

    given, sent = [], []
    for step, chunk in (("give", 0), ("give", 1), ("add", 0), ("give", 2), ("add", 1), ("add", 2)):
        if step == "give":
            part = lax.dynamic_slice(grad, ((1 - core) * half, 0, chunk * some), (half, depth, some))
            grad = after(grad, part)
            given.append(flip(part, "core"))
        else:
            pair = lax.dynamic_slice(grad, (core * half, 0, chunk * some), (half, depth, some)) + given[chunk]
            sent.append(blocks(pair.reshape(half * depth, some).T, ORDERS[chunk][0]))
            grad = after(grad, *sent[-1])
    last = sent[-1]
    nearby = [pltpu.with_memory_space_constraint(a, pltpu.HBM) for a in (weights, first_moment, second_moment)]
    early = last
    for stage in (0, 1):
        sums = []
        for parts, order in zip(sent, ORDERS):
            summed = scatter([after(parts[0], *last)] + parts[1:], order[stage])
            if stage == 0:
                summed = blocks(summed, order[1])
                last = summed
            sums.append(summed)
        sent = sums
    pieces, places = [], []
    for chunk in TOGETHER:
        order = ORDERS[chunk]
        pieces.append(sent[chunk].reshape(SIZES["z"], small, half * depth))
        index = {"y": y, "xh": xh}
        place = (index[order[0]] * SIZES[order[1]] + index[order[1]]) * SIZES["z"] + z
        places.append(after(chunk * some + place * small, *early))
    total = jnp.sum(exchange(jnp.concatenate(pieces, axis=1), "z"), axis=0)
    total = total.reshape(CHUNKS * small, half, depth)

    basis_pair = rows(basis, core, half)
    cut = []
    for moment in (first_moment, second_moment):
        mine = [lax.dynamic_slice(moment, (core * half, 0, at), (half, rank // 2, small)) for at in places]
        cut.append(jnp.swapaxes(jnp.concatenate(mine, axis=2), 1, 2))
    cut = jnp.concatenate(cut, axis=2)
    low, high = in_order(xl, cut, flip(cut, "xl"))
    first = jnp.concatenate([low[:, :, : rank // 2], high[:, :, : rank // 2]], axis=2)
    second = jnp.concatenate([low[:, :, rank // 2 :], high[:, :, rank // 2 :]], axis=2)

    proj = jnp.einsum("fld,ldr->lfr", total, basis_pair, precision=HIGH)
    proj = proj + flip(proj, "xl")
    new_first = 0.9 * first + 0.1 * proj
    new_second = 0.999 * second + 0.001 * proj * proj
    direction = (
        new_first
        / (1.0 - 0.9**ADAM_STEP)
        / (jnp.sqrt(new_second / (1.0 - 0.999**ADAM_STEP)) + 1e-08)
    )
    mine = jnp.where(xl == 0, proj[:, :, : rank // 2], proj[:, :, rank // 2 :])
    packed = jnp.concatenate([direction[0], direction[1], mine[0], mine[1]], axis=1)

    refresh = jnp.einsum("fld,lfr->ldr", total, proj, precision=HIGH)
    refresh = refresh.reshape(2, 2, 2, 3, -1, rank)
    refresh = jnp.transpose(refresh, (2, 1, 0, 3, 4, 5)).reshape(SIZES["z"], 3, -1, rank)
    refresh = jnp.concatenate([refresh[:, i] for i in range(3)], axis=2)
    both = exchange(jnp.concatenate([copies(packed, "z"), refresh], axis=1), "z")
    large = both[:, : 2 * small].reshape(-1, 3 * rank)
    little = both[:, 2 * small : 3 * small].reshape(-1, 3 * rank)
    part = jnp.sum(both[:, 3 * small :], axis=0)

    little = jnp.concatenate([little, part])
    large = gather(large, "xh").reshape(-1, 3 * rank)
    small_y = around(little, "y")
    across = exchange(copies(large, "y"), "y").reshape(-1, 2, small, 3 * rank)
    little = settle(after(little, large), small_y, "y")
    part = jnp.sum(little[:, -part.shape[0] :], axis=0)
    little = little[:, : -part.shape[0]].reshape(-1, 3 * rank)
    part = part + flip(part, "xh")
    little = gather(little, "xh").reshape(-1, 1, small, 3 * rank)

    done = finish((0, 2), [core], [across], basis, *nearby, None)

    refresh = part
    for bit in (2, 1, 0):
        mine, moved = refresh, flip(refresh if bit else after(refresh, little), "z", 1 << bit)
        if bit == 0:
            mine = after(mine, *done)
        refresh = jnp.concatenate(in_order((z >> bit) & 1, mine, moved))
    refresh = refresh.reshape(SIZES["z"], -1, 3 * rank)
    refresh = jnp.stack([refresh[:, :, i * rank : (i + 1) * rank] for i in range(3)], axis=1)
    refresh = refresh.reshape(half, depth, rank)
    gram = jnp.einsum("ldr,lds->lrs", refresh, refresh, precision=HIGH)

    other = flip(across, "core")
    done = finish((0, 2), [1 - core], [after(other, gram)], basis, *nearby, done)
    gram = after(gram, *done) + flip(gram, "xl")
    done = finish((1,), [core, 1 - core], [little, flip(little, "core")], basis, *nearby, done)
    new_weights, new_first, new_second = done
    sumsq = jnp.einsum("lrr->l", gram)
    factor = jnp.sqrt(jnp.float32(rank)) / (2.0 * jnp.sqrt(sumsq + 1e-06))
    scaled = refresh * factor[:, None, None]
    gram_scaled = gram * (factor * factor)[:, None, None]
    basis_new = 1.5 * scaled - 0.5 * jnp.einsum("ldr,lrs->lds", scaled, gram_scaled, precision=HIGH)
    new_basis = jnp.concatenate(in_order(core, after(basis_new, *done), flip(basis_new, "core")), axis=0)
    return (new_weights, new_first, new_second, new_basis)


def solution(mesh):
    fine = Mesh(mesh.devices.reshape(8, 4, 2, 2, 2), ("z", "y", "xh", "core", "xl"))
    split = P(None, "xl", None)
    return jax.shard_map(
        on_device,
        mesh=fine,
        in_specs=(P(REP, None, "xl", None), split, split, split, split),
        out_specs=(split, split, split, split),
        check_vma=False,
    )
```

```python
import functools

import jax
import jax.numpy as jnp
from jax import lax
from jax.experimental import pallas as pl
from jax.experimental.pallas import tpu as pltpu
from jax.sharding import Mesh, PartitionSpec as P

ADAM_STEP = 100
HIGH = lax.Precision.HIGHEST

SIZES = {"z": 8, "y": 4, "xh": 2, "core": 2, "xl": 2}
REP = ("z", "y", "xh", "core")
ORDERS = (("y", "xh"), ("xh", "y"), ("y", "xh"))
CHUNKS = len(ORDERS)
TOGETHER = (0, 2, 1)


def flip(x, axis, bit=1):
    n = SIZES[axis]
    return lax.ppermute(x, axis, [(i, i ^ bit) for i in range(n)])


def rows(x, index, count):
    return lax.dynamic_slice_in_dim(x, index * count, count, 0)


def in_order(index, mine, other):
    first = index == 0
    return jnp.where(first, mine, other), jnp.where(first, other, mine)


def after(x, *others):
    return lax.optimization_barrier((x, *others))[0]


def scatter(parts, axis):
    n = SIZES[axis]
    total = parts[0]
    for k in range(1, n):
        total = total + lax.ppermute(parts[k], axis, [(i, (i + k) % n) for i in range(n)])
    return total


def blocks(x, axis):
    n, me = SIZES[axis], lax.axis_index(axis)
    return [rows(x, (me + k) % n, x.shape[0] // n) for k in range(n)]


def gather(x, axis, own=None):
    n, me = SIZES[axis], lax.axis_index(axis)
    own = x if own is None else own
    if n == 2:
        return jnp.stack(in_order(me, own, flip(x, axis)))
    return settle(own, around(x, axis), axis)


def around(x, axis):
    n = SIZES[axis]
    return [lax.ppermute(x, axis, [(i, (i + k) % n) for i in range(n)]) for k in range(1, n)]


def settle(own, moved, axis):
    n, me = SIZES[axis], lax.axis_index(axis)
    out = jnp.zeros((n,) + own.shape, own.dtype)
    for k, block in enumerate([own] + moved):
        out = lax.dynamic_update_slice_in_dim(out, block[None], (me - k) % n, 0)
    return out


def exchange(parts, axis):
    return lax.all_to_all(parts, axis, split_axis=0, concat_axis=0)


def copies(x, axis):
    return jnp.broadcast_to(x, (SIZES[axis],) + x.shape)


def finish_kernel(chunks, count, *refs):
    pairs, *sources = refs[: 1 + count]
    basis, weights, first, second = refs[1 + count : 5 + count]
    outs, (x, w, f, s, x_sem, in_sem, out_sem) = refs[-10:-7], refs[-7:]
    rank, some = basis.shape[2], w.shape[2]
    steps = [(h, k, j) for h in range(len(chunks)) for k in range(count) for j in range(2)]
    loads, reads, writes = [], [], []
    for i, (h, k, j) in enumerate(steps):
        if j == 0:
            loads.append(pltpu.make_async_copy(sources[k].at[:, h], x.at[i // 2], x_sem.at[i // 2]))
            loads[-1].start()
        layer, columns = pairs[k] * 2 + j, pl.ds(chunks[h] * some, some)
        far = [a.at[layer, :, columns] for a in (weights, first, second, *outs)]
        near = [a.at[i] for a in (w, f, s)]
        reads.append([pltpu.make_async_copy(far[n], near[n], in_sem.at[i, n]) for n in range(3)])
        writes.append([pltpu.make_async_copy(near[n], far[3 + n], out_sem.at[i, n]) for n in range(3)])
        for copy in reads[-1]:
            copy.start()
    for i, (h, k, j) in enumerate(steps):
        if j == 0:
            loads[i // 2].wait()
            both = x[i // 2, :, :, 2 * rank :].reshape(some, rank).T
        for copy in reads[i]:
            copy.wait()
        direction = x[i // 2, :, :, j * rank : (j + 1) * rank].reshape(some, rank)
        update = lax.dot_general(
            basis[pairs[k] * 2 + j],
            direction,
            (((1,), (1,)), ((), ())),
            precision=HIGH,
            preferred_element_type=jnp.float32,
        )
        w[i] = w[i] - 0.0125 * update
        proj = both[j * rank // 2 : (j + 1) * rank // 2]
        f[i] = 0.9 * f[i] + 0.1 * proj
        s[i] = 0.999 * s[i] + 0.001 * proj * proj
        for copy in writes[i]:
            copy.start()
    for copies_out in writes:
        for copy in copies_out:
            copy.wait()


def finish(chunks, pairs, sources, basis, weights, first, second, before):
    layers, depth, width = weights.shape
    rank, some = basis.shape[2], width // CHUNKS
    count = len(sources)
    steps = 2 * count * len(chunks)
    far = pl.BlockSpec(memory_space=pl.ANY)
    kept = [] if before is None else list(before)
    low = pltpu.VMEM((steps, first.shape[1], some), first.dtype)
    return pl.pallas_call(
        functools.partial(finish_kernel, chunks, count),
        in_specs=[pl.BlockSpec(memory_space=pltpu.SMEM)]
        + [far] * count
        + [pl.BlockSpec(memory_space=pltpu.VMEM)]
        + [far] * (3 + len(kept)),
        out_specs=[far] * 3,
        out_shape=[jax.ShapeDtypeStruct(a.shape, a.dtype) for a in (weights, first, second)],
        input_output_aliases={5 + count + i: i for i in range(len(kept))},
        scratch_shapes=[
            pltpu.VMEM((steps // 2,) + sources[0].shape[:1] + sources[0].shape[2:], weights.dtype),
            pltpu.VMEM((steps, depth, some), weights.dtype),
            low,
            low,
            pltpu.SemaphoreType.DMA((steps // 2,)),
            pltpu.SemaphoreType.DMA((steps, 3)),
            pltpu.SemaphoreType.DMA((steps, 3)),
        ],
        compiler_params=pltpu.CompilerParams(vmem_limit_bytes=20 << 20),
        cost_estimate=pl.CostEstimate(
            flops=12 * steps * depth * rank * some, bytes_accessed=8 * steps * (depth + rank) * some, transcendentals=0
        ),
        name="finish",
    )(jnp.stack(pairs), *sources, basis, weights, first, second, *kept)


def on_device(grads, basis, weights, first_moment, second_moment):
    layers, depth, width = grads.shape[1:]
    rank = basis.shape[2]
    half = layers // 2
    some = width // CHUNKS
    small = some // 64
    z, y, xh = lax.axis_index("z"), lax.axis_index("y"), lax.axis_index("xh")
    core, xl = lax.axis_index("core"), lax.axis_index("xl")
    grad = grads[0]

    given, sent = [], []
    for step, chunk in (("give", 0), ("give", 1), ("add", 0), ("give", 2), ("add", 1), ("add", 2)):
        if step == "give":
            part = lax.dynamic_slice(grad, ((1 - core) * half, 0, chunk * some), (half, depth, some))
            grad = after(grad, part)
            given.append(flip(part, "core"))
        else:
            pair = lax.dynamic_slice(grad, (core * half, 0, chunk * some), (half, depth, some)) + given[chunk]
            sent.append(blocks(pair.reshape(half * depth, some).T, ORDERS[chunk][0]))
            grad = after(grad, *sent[-1])
    last = sent[-1]
    nearby = [pltpu.with_memory_space_constraint(a, pltpu.HBM) for a in (weights, first_moment, second_moment)]
    early = last
    for stage in (0, 1):
        sums = []
        for parts, order in zip(sent, ORDERS):
            summed = scatter([after(parts[0], *last)] + parts[1:], order[stage])
            if stage == 0:
                summed = blocks(summed, order[1])
                last = summed
            sums.append(summed)
        sent = sums
    pieces, places = [], []
    for chunk in TOGETHER:
        order = ORDERS[chunk]
        pieces.append(sent[chunk].reshape(SIZES["z"], small, half * depth))
        index = {"y": y, "xh": xh}
        place = (index[order[0]] * SIZES[order[1]] + index[order[1]]) * SIZES["z"] + z
        places.append(after(chunk * some + place * small, *early))
    total = jnp.sum(exchange(jnp.concatenate(pieces, axis=1), "z"), axis=0)
    total = total.reshape(CHUNKS * small, half, depth)

    basis_pair = rows(basis, core, half)
    cut = []
    for moment in (first_moment, second_moment):
        mine = [lax.dynamic_slice(moment, (core * half, 0, at), (half, rank // 2, small)) for at in places]
        cut.append(jnp.swapaxes(jnp.concatenate(mine, axis=2), 1, 2))
    cut = jnp.concatenate(cut, axis=2)
    low, high = in_order(xl, cut, flip(cut, "xl"))
    first = jnp.concatenate([low[:, :, : rank // 2], high[:, :, : rank // 2]], axis=2)
    second = jnp.concatenate([low[:, :, rank // 2 :], high[:, :, rank // 2 :]], axis=2)

    proj = jnp.einsum("fld,ldr->lfr", total, basis_pair, precision=HIGH)
    proj = proj + flip(proj, "xl")
    new_first = 0.9 * first + 0.1 * proj
    new_second = 0.999 * second + 0.001 * proj * proj
    direction = (
        new_first
        / (1.0 - 0.9**ADAM_STEP)
        / (jnp.sqrt(new_second / (1.0 - 0.999**ADAM_STEP)) + 1e-08)
    )
    mine = jnp.where(xl == 0, proj[:, :, : rank // 2], proj[:, :, rank // 2 :])
    packed = jnp.concatenate([direction[0], direction[1], mine[0], mine[1]], axis=1)

    refresh = jnp.einsum("fld,lfr->ldr", total, proj, precision=HIGH)
    refresh = refresh.reshape(2, 2, 2, 3, -1, rank)
    refresh = jnp.transpose(refresh, (2, 1, 0, 3, 4, 5)).reshape(SIZES["z"], 3, -1, rank)
    refresh = jnp.concatenate([refresh[:, i] for i in range(3)], axis=2)
    both = exchange(jnp.concatenate([copies(packed, "z"), refresh], axis=1), "z")
    large = both[:, : 2 * small].reshape(-1, 3 * rank)
    little = both[:, 2 * small : 3 * small].reshape(-1, 3 * rank)
    part = jnp.sum(both[:, 3 * small :], axis=0)

    little = jnp.concatenate([little, part])
    large = gather(large, "xh").reshape(-1, 3 * rank)
    small_y = around(little, "y")
    across = exchange(copies(large, "y"), "y").reshape(-1, 2, small, 3 * rank)
    little = settle(after(little, large), small_y, "y")
    part = jnp.sum(little[:, -part.shape[0] :], axis=0)
    little = little[:, : -part.shape[0]].reshape(-1, 3 * rank)
    part = part + flip(part, "xh")
    little = gather(little, "xh").reshape(-1, 1, small, 3 * rank)

    done = finish((0, 2), [core], [across], basis, *nearby, None)

    refresh = part
    for bit in (2, 1, 0):
        mine, moved = refresh, flip(refresh if bit else after(refresh, little), "z", 1 << bit)
        if bit == 0:
            mine = after(mine, *done)
        refresh = jnp.concatenate(in_order((z >> bit) & 1, mine, moved))
    refresh = refresh.reshape(SIZES["z"], -1, 3 * rank)
    refresh = jnp.stack([refresh[:, :, i * rank : (i + 1) * rank] for i in range(3)], axis=1)
    refresh = refresh.reshape(half, depth, rank)
    gram = jnp.einsum("ldr,lds->lrs", refresh, refresh, precision=HIGH)

    other = flip(across, "core")
    done = finish((0, 2), [1 - core], [after(other, gram)], basis, *nearby, done)
    gram = after(gram, *done) + flip(gram, "xl")
    done = finish((1,), [core, 1 - core], [little, flip(little, "core")], basis, *nearby, done)
    new_weights, new_first, new_second = done
    sumsq = jnp.einsum("lrr->l", gram)
    factor = jnp.sqrt(jnp.float32(rank)) / (2.0 * jnp.sqrt(sumsq + 1e-06))
    scaled = refresh * factor[:, None, None]
    gram_scaled = gram * (factor * factor)[:, None, None]
    basis_new = 1.5 * scaled - 0.5 * jnp.einsum("ldr,lrs->lds", scaled, gram_scaled, precision=HIGH)
    new_basis = jnp.concatenate(in_order(core, after(basis_new, *done), flip(basis_new, "core")), axis=0)
    return (new_weights, new_first, new_second, new_basis)


def solution(mesh):
    fine = Mesh(mesh.devices.reshape(8, 4, 2, 2, 2), ("z", "y", "xh", "core", "xl"))
    split = P(None, "xl", None)
    return jax.shard_map(
        on_device,
        mesh=fine,
        in_specs=(P(REP, None, "xl", None), split, split, split, split),
        out_specs=(split, split, split, split),
        check_vma=False,
    )
```

```python
import functools

import jax
import jax.numpy as jnp
from jax import lax
from jax.experimental import pallas as pl
from jax.experimental.pallas import tpu as pltpu
from jax.sharding import Mesh, PartitionSpec as P

ADAM_STEP = 100
HIGH = lax.Precision.HIGHEST

SIZES = {"z": 8, "y": 4, "xh": 2, "core": 2, "xl": 2}
REP = ("z", "y", "xh", "core")
ORDERS = (("y", "xh"), ("xh", "y"), ("y", "xh"))
CHUNKS = len(ORDERS)
TOGETHER = (0, 2, 1)


def flip(x, axis, bit=1):
    n = SIZES[axis]
    return lax.ppermute(x, axis, [(i, i ^ bit) for i in range(n)])


def rows(x, index, count):
    return lax.dynamic_slice_in_dim(x, index * count, count, 0)


def in_order(index, mine, other):
    first = index == 0
    return jnp.where(first, mine, other), jnp.where(first, other, mine)


def after(x, *others):
    return lax.optimization_barrier((x, *others))[0]


def scatter(parts, axis):
    n = SIZES[axis]
    total = parts[0]
    for k in range(1, n):
        total = total + lax.ppermute(parts[k], axis, [(i, (i + k) % n) for i in range(n)])
    return total


def blocks(x, axis):
    n, me = SIZES[axis], lax.axis_index(axis)
    return [rows(x, (me + k) % n, x.shape[0] // n) for k in range(n)]


def gather(x, axis, own=None):
    n, me = SIZES[axis], lax.axis_index(axis)
    own = x if own is None else own
    if n == 2:
        return jnp.stack(in_order(me, own, flip(x, axis)))
    return settle(own, around(x, axis), axis)


def around(x, axis):
    n = SIZES[axis]
    return [lax.ppermute(x, axis, [(i, (i + k) % n) for i in range(n)]) for k in range(1, n)]


def settle(own, moved, axis):
    n, me = SIZES[axis], lax.axis_index(axis)
    out = jnp.zeros((n,) + own.shape, own.dtype)
    for k, block in enumerate([own] + moved):
        out = lax.dynamic_update_slice_in_dim(out, block[None], (me - k) % n, 0)
    return out


def exchange(parts, axis):
    return lax.all_to_all(parts, axis, split_axis=0, concat_axis=0)


def copies(x, axis):
    return jnp.broadcast_to(x, (SIZES[axis],) + x.shape)


def finish_kernel(chunks, count, *refs):
    pairs, *sources = refs[: 1 + count]
    basis, weights, first, second = refs[1 + count : 5 + count]
    outs, (x, w, f, s, x_sem, in_sem, out_sem) = refs[-10:-7], refs[-7:]
    rank, some = basis.shape[2], w.shape[2]
    steps = [(h, k, j) for h in range(len(chunks)) for k in range(count) for j in range(2)]
    loads, reads, writes = [], [], []
    for i, (h, k, j) in enumerate(steps):
        if j == 0:
            loads.append(pltpu.make_async_copy(sources[k].at[:, h], x.at[i // 2], x_sem.at[i // 2]))
            loads[-1].start()
        layer, columns = pairs[k] * 2 + j, pl.ds(chunks[h] * some, some)
        far = [a.at[layer, :, columns] for a in (weights, first, second, *outs)]
        near = [a.at[i] for a in (w, f, s)]
        reads.append([pltpu.make_async_copy(far[n], near[n], in_sem.at[i, n]) for n in range(3)])
        writes.append([pltpu.make_async_copy(near[n], far[3 + n], out_sem.at[i, n]) for n in range(3)])
        for copy in reads[-1]:
            copy.start()
    for i, (h, k, j) in enumerate(steps):
        if j == 0:
            loads[i // 2].wait()
            both = x[i // 2, :, :, 2 * rank :].reshape(some, rank).T
        for copy in reads[i]:
            copy.wait()
        direction = x[i // 2, :, :, j * rank : (j + 1) * rank].reshape(some, rank)
        update = lax.dot_general(
            basis[pairs[k] * 2 + j],
            direction,
            (((1,), (1,)), ((), ())),
            precision=HIGH,
            preferred_element_type=jnp.float32,
        )
        w[i] = w[i] - 0.0125 * update
        proj = both[j * rank // 2 : (j + 1) * rank // 2]
        f[i] = 0.9 * f[i] + 0.1 * proj
        s[i] = 0.999 * s[i] + 0.001 * proj * proj
        for copy in writes[i]:
            copy.start()
    for copies_out in writes:
        for copy in copies_out:
            copy.wait()


def finish(chunks, pairs, sources, basis, weights, first, second, before):
    layers, depth, width = weights.shape
    rank, some = basis.shape[2], width // CHUNKS
    count = len(sources)
    steps = 2 * count * len(chunks)
    far = pl.BlockSpec(memory_space=pl.ANY)
    kept = [] if before is None else list(before)
    low = pltpu.VMEM((steps, first.shape[1], some), first.dtype)
    return pl.pallas_call(
        functools.partial(finish_kernel, chunks, count),
        in_specs=[pl.BlockSpec(memory_space=pltpu.SMEM)]
        + [far] * count
        + [pl.BlockSpec(memory_space=pltpu.VMEM)]
        + [far] * (3 + len(kept)),
        out_specs=[far] * 3,
        out_shape=[jax.ShapeDtypeStruct(a.shape, a.dtype) for a in (weights, first, second)],
        input_output_aliases={5 + count + i: i for i in range(len(kept))},
        scratch_shapes=[
            pltpu.VMEM((steps // 2,) + sources[0].shape[:1] + sources[0].shape[2:], weights.dtype),
            pltpu.VMEM((steps, depth, some), weights.dtype),
            low,
            low,
            pltpu.SemaphoreType.DMA((steps // 2,)),
            pltpu.SemaphoreType.DMA((steps, 3)),
            pltpu.SemaphoreType.DMA((steps, 3)),
        ],
        compiler_params=pltpu.CompilerParams(vmem_limit_bytes=20 << 20),
        cost_estimate=pl.CostEstimate(
            flops=0, bytes_accessed=0, transcendentals=0
        ),
        name="finish",
    )(jnp.stack(pairs), *sources, basis, weights, first, second, *kept)


def on_device(grads, basis, weights, first_moment, second_moment):
    layers, depth, width = grads.shape[1:]
    rank = basis.shape[2]
    half = layers // 2
    some = width // CHUNKS
    small = some // 64
    z, y, xh = lax.axis_index("z"), lax.axis_index("y"), lax.axis_index("xh")
    core, xl = lax.axis_index("core"), lax.axis_index("xl")
    grad = grads[0]

    given, sent = [], []
    for step, chunk in (("give", 0), ("give", 1), ("add", 0), ("give", 2), ("add", 1), ("add", 2)):
        if step == "give":
            part = lax.dynamic_slice(grad, ((1 - core) * half, 0, chunk * some), (half, depth, some))
            grad = after(grad, part)
            given.append(flip(part, "core"))
        else:
            pair = lax.dynamic_slice(grad, (core * half, 0, chunk * some), (half, depth, some)) + given[chunk]
            sent.append(blocks(pair.reshape(half * depth, some).T, ORDERS[chunk][0]))
            grad = after(grad, *sent[-1])
    last = sent[-1]
    nearby = [pltpu.with_memory_space_constraint(a, pltpu.HBM) for a in (weights, first_moment, second_moment)]
    early = last
    for stage in (0, 1):
        sums = []
        for parts, order in zip(sent, ORDERS):
            summed = scatter([after(parts[0], *last)] + parts[1:], order[stage])
            if stage == 0:
                summed = blocks(summed, order[1])
                last = summed
            sums.append(summed)
        sent = sums
    pieces, places = [], []
    for chunk in TOGETHER:
        order = ORDERS[chunk]
        pieces.append(sent[chunk].reshape(SIZES["z"], small, half * depth))
        index = {"y": y, "xh": xh}
        place = (index[order[0]] * SIZES[order[1]] + index[order[1]]) * SIZES["z"] + z
        places.append(after(chunk * some + place * small, *early))
    total = jnp.sum(exchange(jnp.concatenate(pieces, axis=1), "z"), axis=0)
    total = total.reshape(CHUNKS * small, half, depth)

    basis_pair = rows(basis, core, half)
    cut = []
    for moment in (first_moment, second_moment):
        mine = [lax.dynamic_slice(moment, (core * half, 0, at), (half, rank // 2, small)) for at in places]
        cut.append(jnp.swapaxes(jnp.concatenate(mine, axis=2), 1, 2))
    cut = jnp.concatenate(cut, axis=2)
    low, high = in_order(xl, cut, flip(cut, "xl"))
    first = jnp.concatenate([low[:, :, : rank // 2], high[:, :, : rank // 2]], axis=2)
    second = jnp.concatenate([low[:, :, rank // 2 :], high[:, :, rank // 2 :]], axis=2)

    proj = jnp.einsum("fld,ldr->lfr", total, basis_pair, precision=HIGH)
    proj = proj + flip(proj, "xl")
    new_first = 0.9 * first + 0.1 * proj
    new_second = 0.999 * second + 0.001 * proj * proj
    direction = (
        new_first
        / (1.0 - 0.9**ADAM_STEP)
        / (jnp.sqrt(new_second / (1.0 - 0.999**ADAM_STEP)) + 1e-08)
    )
    mine = jnp.where(xl == 0, proj[:, :, : rank // 2], proj[:, :, rank // 2 :])
    packed = jnp.concatenate([direction[0], direction[1], mine[0], mine[1]], axis=1)

    refresh = jnp.einsum("fld,lfr->ldr", total, proj, precision=HIGH)
    refresh = refresh.reshape(2, 2, 2, 3, -1, rank)
    refresh = jnp.transpose(refresh, (2, 1, 0, 3, 4, 5)).reshape(SIZES["z"], 3, -1, rank)
    refresh = jnp.concatenate([refresh[:, i] for i in range(3)], axis=2)
    both = exchange(jnp.concatenate([copies(packed, "z"), refresh], axis=1), "z")
    large = both[:, : 2 * small].reshape(-1, 3 * rank)
    little = both[:, 2 * small : 3 * small].reshape(-1, 3 * rank)
    part = jnp.sum(both[:, 3 * small :], axis=0)

    little = jnp.concatenate([little, part])
    large = gather(large, "xh").reshape(-1, 3 * rank)
    small_y = around(little, "y")
    across = exchange(copies(large, "y"), "y").reshape(-1, 2, small, 3 * rank)
    little = settle(after(little, large), small_y, "y")
    part = jnp.sum(little[:, -part.shape[0] :], axis=0)
    little = little[:, : -part.shape[0]].reshape(-1, 3 * rank)
    part = part + flip(part, "xh")
    little = gather(little, "xh").reshape(-1, 1, small, 3 * rank)
    done = finish((1,), [core, 1 - core], [little, flip(little, "core")], basis, *nearby, None)

    refresh = part
    for bit in (2, 1, 0):
        mine, moved = refresh, flip(after(refresh, little) if bit == 1 else refresh, "z", 1 << bit)
        if bit == 0:
            mine = after(mine, *done)
        refresh = jnp.concatenate(in_order((z >> bit) & 1, mine, moved))
    refresh = refresh.reshape(SIZES["z"], -1, 3 * rank)
    refresh = jnp.stack([refresh[:, :, i * rank : (i + 1) * rank] for i in range(3)], axis=1)
    refresh = refresh.reshape(half, depth, rank)
    gram = jnp.einsum("ldr,lds->lrs", refresh, refresh, precision=HIGH)
    across = after(across, *done)
    other = flip(across, "core")
    done = finish((0, 2), [core], [after(across, gram)], basis, *nearby, done)
    gram = after(gram, *done) + flip(gram, "xl")
    sumsq = jnp.einsum("lrr->l", gram)
    factor = jnp.sqrt(jnp.float32(rank)) / (2.0 * jnp.sqrt(sumsq + 1e-06))
    scaled = refresh * factor[:, None, None]
    gram_scaled = gram * (factor * factor)[:, None, None]
    basis_new = 1.5 * scaled - 0.5 * jnp.einsum("ldr,lrs->lds", scaled, gram_scaled, precision=HIGH)
    moved = flip(basis_new, "core")
    done = finish((0, 2), [1 - core], [after(other, basis_new)], basis, *nearby, done)
    new_weights, new_first, new_second = done
    new_basis = jnp.concatenate(in_order(core, after(basis_new, *done), moved), axis=0)
    return (new_weights, new_first, new_second, new_basis)


def solution(mesh):
    fine = Mesh(mesh.devices.reshape(8, 4, 2, 2, 2), ("z", "y", "xh", "core", "xl"))
    split = P(None, "xl", None)
    return jax.shard_map(
        on_device,
        mesh=fine,
        in_specs=(P(REP, None, "xl", None), split, split, split, split),
        out_specs=(split, split, split, split),
        check_vma=False,
    )
```

```python
import functools

import jax
import jax.numpy as jnp
from jax import lax
from jax.experimental import pallas as pl
from jax.experimental.pallas import tpu as pltpu
from jax.sharding import Mesh, PartitionSpec as P

ADAM_STEP = 100
HIGH = lax.Precision.HIGHEST

SIZES = {"z": 8, "y": 4, "xh": 2, "core": 2, "xl": 2}
REP = ("z", "y", "xh", "core")
ORDERS = (("y", "xh"), ("xh", "y"), ("y", "xh"))
CHUNKS = len(ORDERS)
TOGETHER = (0, 2, 1)


def flip(x, axis, bit=1):
    n = SIZES[axis]
    return lax.ppermute(x, axis, [(i, i ^ bit) for i in range(n)])


def rows(x, index, count):
    return lax.dynamic_slice_in_dim(x, index * count, count, 0)


def in_order(index, mine, other):
    first = index == 0
    return jnp.where(first, mine, other), jnp.where(first, other, mine)


def after(x, *others):
    return lax.optimization_barrier((x, *others))[0]


def scatter(parts, axis):
    n = SIZES[axis]
    total = parts[0]
    for k in range(1, n):
        total = total + lax.ppermute(parts[k], axis, [(i, (i + k) % n) for i in range(n)])
    return total


def blocks(x, axis):
    n, me = SIZES[axis], lax.axis_index(axis)
    return [rows(x, (me + k) % n, x.shape[0] // n) for k in range(n)]


def gather(x, axis, own=None):
    n, me = SIZES[axis], lax.axis_index(axis)
    own = x if own is None else own
    if n == 2:
        return jnp.stack(in_order(me, own, flip(x, axis)))
    return settle(own, around(x, axis), axis)


def around(x, axis):
    n = SIZES[axis]
    return [lax.ppermute(x, axis, [(i, (i + k) % n) for i in range(n)]) for k in range(1, n)]


def settle(own, moved, axis):
    n, me = SIZES[axis], lax.axis_index(axis)
    out = jnp.zeros((n,) + own.shape, own.dtype)
    for k, block in enumerate([own] + moved):
        out = lax.dynamic_update_slice_in_dim(out, block[None], (me - k) % n, 0)
    return out


def exchange(parts, axis):
    return lax.all_to_all(parts, axis, split_axis=0, concat_axis=0)


def copies(x, axis):
    return jnp.broadcast_to(x, (SIZES[axis],) + x.shape)


def finish_kernel(chunks, count, *refs):
    pairs, *sources = refs[: 1 + count]
    basis, weights, first, second = refs[1 + count : 5 + count]
    outs, (x, w, f, s, x_sem, in_sem, out_sem) = refs[-10:-7], refs[-7:]
    rank, some = basis.shape[2], w.shape[2]
    steps = [(h, k, j) for h in range(len(chunks)) for k in range(count) for j in range(2)]
    loads, reads, writes = [], [], []
    for i, (h, k, j) in enumerate(steps):
        if j == 0:
            loads.append(pltpu.make_async_copy(sources[k].at[:, h], x.at[i // 2], x_sem.at[i // 2]))
            loads[-1].start()
        layer, columns = pairs[k] * 2 + j, pl.ds(chunks[h] * some, some)
        far = [a.at[layer, :, columns] for a in (weights, first, second, *outs)]
        near = [a.at[i] for a in (w, f, s)]
        reads.append([pltpu.make_async_copy(far[n], near[n], in_sem.at[i, n]) for n in range(3)])
        writes.append([pltpu.make_async_copy(near[n], far[3 + n], out_sem.at[i, n]) for n in range(3)])
        for copy in reads[-1]:
            copy.start()
    for i, (h, k, j) in enumerate(steps):
        if j == 0:
            loads[i // 2].wait()
            both = x[i // 2, :, :, 2 * rank :].reshape(some, rank).T
        for copy in reads[i]:
            copy.wait()
        direction = x[i // 2, :, :, j * rank : (j + 1) * rank].reshape(some, rank)
        update = lax.dot_general(
            basis[pairs[k] * 2 + j],
            direction,
            (((1,), (1,)), ((), ())),
            precision=HIGH,
            preferred_element_type=jnp.float32,
        )
        w[i] = w[i] - 0.0125 * update
        proj = both[j * rank // 2 : (j + 1) * rank // 2]
        f[i] = 0.9 * f[i] + 0.1 * proj
        s[i] = 0.999 * s[i] + 0.001 * proj * proj
        for copy in writes[i]:
            copy.start()
    for copies_out in writes:
        for copy in copies_out:
            copy.wait()


def finish(chunks, pairs, sources, basis, weights, first, second, before):
    layers, depth, width = weights.shape
    rank, some = basis.shape[2], width // CHUNKS
    count = len(sources)
    steps = 2 * count * len(chunks)
    far = pl.BlockSpec(memory_space=pl.ANY)
    kept = [] if before is None else list(before)
    low = pltpu.VMEM((steps, first.shape[1], some), first.dtype)
    return pl.pallas_call(
        functools.partial(finish_kernel, chunks, count),
        in_specs=[pl.BlockSpec(memory_space=pltpu.SMEM)]
        + [far] * count
        + [pl.BlockSpec(memory_space=pltpu.VMEM)]
        + [far] * (3 + len(kept)),
        out_specs=[far] * 3,
        out_shape=[jax.ShapeDtypeStruct(a.shape, a.dtype) for a in (weights, first, second)],
        input_output_aliases={5 + count + i: i for i in range(len(kept))},
        scratch_shapes=[
            pltpu.VMEM((steps // 2,) + sources[0].shape[:1] + sources[0].shape[2:], weights.dtype),
            pltpu.VMEM((steps, depth, some), weights.dtype),
            low,
            low,
            pltpu.SemaphoreType.DMA((steps // 2,)),
            pltpu.SemaphoreType.DMA((steps, 3)),
            pltpu.SemaphoreType.DMA((steps, 3)),
        ],
        compiler_params=pltpu.CompilerParams(vmem_limit_bytes=20 << 20),
        cost_estimate=pl.CostEstimate(
            flops=12 * steps * depth * rank * some, bytes_accessed=8 * steps * (depth + rank) * some, transcendentals=0
        ),
        name="finish",
    )(jnp.stack(pairs), *sources, basis, weights, first, second, *kept)


def on_device(grads, basis, weights, first_moment, second_moment):
    layers, depth, width = grads.shape[1:]
    rank = basis.shape[2]
    half = layers // 2
    some = width // CHUNKS
    small = some // 64
    z, y, xh = lax.axis_index("z"), lax.axis_index("y"), lax.axis_index("xh")
    core, xl = lax.axis_index("core"), lax.axis_index("xl")
    grad = grads[0]

    given, sent = [], []
    for step, chunk in (("give", 0), ("give", 1), ("add", 0), ("add", 1), ("give", 2), ("add", 2)):
        if step == "give":
            part = lax.dynamic_slice(grad, ((1 - core) * half, 0, chunk * some), (half, depth, some))
            grad = after(grad, part)
            given.append(flip(part, "core"))
        else:
            pair = lax.dynamic_slice(grad, (core * half, 0, chunk * some), (half, depth, some)) + given[chunk]
            sent.append(blocks(pair.reshape(half * depth, some).T, ORDERS[chunk][0]))
            grad = after(grad, *sent[-1])
    last = sent[-1]
    nearby = [pltpu.with_memory_space_constraint(a, pltpu.HBM) for a in (weights, first_moment, second_moment)]
    early = last
    for stage in (0, 1):
        sums = []
        for parts, order in zip(sent, ORDERS):
            summed = scatter([after(parts[0], *last)] + parts[1:], order[stage])
            if stage == 0:
                summed = blocks(summed, order[1])
                last = summed
            sums.append(summed)
        sent = sums
    pieces, places = [], []
    for chunk in TOGETHER:
        order = ORDERS[chunk]
        pieces.append(sent[chunk].reshape(SIZES["z"], small, half * depth))
        index = {"y": y, "xh": xh}
        place = (index[order[0]] * SIZES[order[1]] + index[order[1]]) * SIZES["z"] + z
        places.append(after(chunk * some + place * small, *early))
    total = jnp.sum(exchange(jnp.concatenate(pieces, axis=1), "z"), axis=0)
    total = total.reshape(CHUNKS * small, half, depth)

    basis_pair = rows(basis, core, half)
    cut = []
    for moment in (first_moment, second_moment):
        mine = [lax.dynamic_slice(moment, (core * half, 0, at), (half, rank // 2, small)) for at in places]
        cut.append(jnp.swapaxes(jnp.concatenate(mine, axis=2), 1, 2))
    cut = jnp.concatenate(cut, axis=2)
    low, high = in_order(xl, cut, flip(cut, "xl"))
    first = jnp.concatenate([low[:, :, : rank // 2], high[:, :, : rank // 2]], axis=2)
    second = jnp.concatenate([low[:, :, rank // 2 :], high[:, :, rank // 2 :]], axis=2)

    proj = jnp.einsum("fld,ldr->lfr", total, basis_pair, precision=HIGH)
    proj = proj + flip(proj, "xl")
    new_first = 0.9 * first + 0.1 * proj
    new_second = 0.999 * second + 0.001 * proj * proj
    direction = (
        new_first
        / (1.0 - 0.9**ADAM_STEP)
        / (jnp.sqrt(new_second / (1.0 - 0.999**ADAM_STEP)) + 1e-08)
    )
    mine = jnp.where(xl == 0, proj[:, :, : rank // 2], proj[:, :, rank // 2 :])
    packed = jnp.concatenate([direction[0], direction[1], mine[0], mine[1]], axis=1)

    refresh = jnp.einsum("fld,lfr->ldr", total, proj, precision=HIGH)
    refresh = refresh.reshape(2, 2, 2, 3, -1, rank)
    refresh = jnp.transpose(refresh, (2, 1, 0, 3, 4, 5)).reshape(SIZES["z"], 3, -1, rank)
    refresh = jnp.concatenate([refresh[:, i] for i in range(3)], axis=2)
    both = exchange(jnp.concatenate([copies(packed, "z"), refresh], axis=1), "z")
    large = both[:, : 2 * small].reshape(-1, 3 * rank)
    little = both[:, 2 * small : 3 * small].reshape(-1, 3 * rank)
    part = jnp.sum(both[:, 3 * small :], axis=0)

    little = jnp.concatenate([little, part])
    large = gather(large, "xh").reshape(-1, 3 * rank)
    small_y = around(little, "y")
    across = exchange(copies(large, "y"), "y").reshape(-1, 2, small, 3 * rank)
    little = settle(after(little, large), small_y, "y")
    part = jnp.sum(little[:, -part.shape[0] :], axis=0)
    little = little[:, : -part.shape[0]].reshape(-1, 3 * rank)
    part = part + flip(part, "xh")
    little = gather(little, "xh").reshape(-1, 1, small, 3 * rank)

    done = finish((0, 2), [core], [across], basis, *nearby, None)

    refresh = part
    for bit in (2, 1, 0):
        mine, moved = refresh, flip(refresh if bit else after(refresh, little), "z", 1 << bit)
        if bit == 0:
            mine = after(mine, *done)
        refresh = jnp.concatenate(in_order((z >> bit) & 1, mine, moved))
    refresh = refresh.reshape(SIZES["z"], -1, 3 * rank)
    refresh = jnp.stack([refresh[:, :, i * rank : (i + 1) * rank] for i in range(3)], axis=1)
    refresh = refresh.reshape(half, depth, rank)
    gram = jnp.einsum("ldr,lds->lrs", refresh, refresh, precision=HIGH)

    other = flip(across, "core")
    done = finish((0, 2), [1 - core], [after(other, gram)], basis, *nearby, done)
    gram = after(gram, *done) + flip(gram, "xl")
    done = finish((1,), [core, 1 - core], [little, flip(little, "core")], basis, *nearby, done)
    new_weights, new_first, new_second = done
    sumsq = jnp.einsum("lrr->l", gram)
    factor = jnp.sqrt(jnp.float32(rank)) / (2.0 * jnp.sqrt(sumsq + 1e-06))
    scaled = refresh * factor[:, None, None]
    gram_scaled = gram * (factor * factor)[:, None, None]
    basis_new = 1.5 * scaled - 0.5 * jnp.einsum("ldr,lrs->lds", scaled, gram_scaled, precision=HIGH)
    new_basis = jnp.concatenate(in_order(core, after(basis_new, *done), flip(basis_new, "core")), axis=0)
    return (new_weights, new_first, new_second, new_basis)


def solution(mesh):
    fine = Mesh(mesh.devices.reshape(8, 4, 2, 2, 2), ("z", "y", "xh", "core", "xl"))
    split = P(None, "xl", None)
    return jax.shard_map(
        on_device,
        mesh=fine,
        in_specs=(P(REP, None, "xl", None), split, split, split, split),
        out_specs=(split, split, split, split),
        check_vma=False,
    )
```
